32 devices in a mesh: hi: 8 (over y, x, core), lo: 4 (over z).
Axes of the slice: x: 2, y: 2, z: 4, core: 2. Of those that a mesh axis runs over, the one named last changes fastest.
Arguments:
- track: float32 [8192, 512], P(('hi', 'lo')), may hold values from -6 to 6
- tight_weight: float32 [1536, 512], replicated, may hold values from -0.15625 to 0.15625
- wide_weight: float32 [1536, 512], replicated, may hold values from -0.15625 to 0.15625
- cotangent: float32 [8192, 512], P(('hi', 'lo')), may hold values from -6 to 6
Outputs:
- features_out: float32 [8192, 512], P(('hi', 'lo'))
- grad_track: float32 [8192, 512], P(('hi', 'lo'))
- grad_near: float32 [1536, 512], P('lo')
- grad_far: float32 [1536, 512], P('lo')
The draws below stay inside these ranges and needn't reach their ends.
All inputs are finite; a program needn't handle non-finite values.
Results may differ from the reference program's by a relative error of at most 0.000073.
Values sent between devices are 32-bit elements; how exact they have to be, the bound alone decides.
No kernel may reach another device: no remote copies, remote signals or barrier semaphores. Data moves between devices by JAX's collectives and lax.ppermute only.
A program may use at most 64 MiB of HBM per device.

```python
import jax
import jax.numpy as jnp
from jax import lax

C = 512
LENGTH = 8192
TIGHT_DILATION = 1024
WIDE_DILATION = 2048


def levels(own_key, dims, pieces, least, top_value):
    level = 1.0
    for dim, blocks in pieces:
        steps = jax.random.uniform(jax.random.fold_in(jax.random.fold_in(own_key, 6), dim), (blocks,), jnp.float32, least / len(pieces), top_value / len(pieces))
        level = level * jnp.repeat(jnp.exp(steps), dims[dim] // blocks).reshape((-1,) + (1,) * (len(dims) - 1 - dim))
    return level


def normal_values(rng, dims, deviation, most, shards=(), dtype=jnp.bfloat16):
    drawn = jax.random.normal(rng, dims, jnp.float32) * deviation
    if len(shards) > 0:
        drawn = levels(rng, dims, shards, -0.22, 0.18) * drawn
    return jnp.clip(drawn, min=-most, max=most).astype(dtype)


def setup_inputs(seed: int = 0) -> dict:
    seeds = jax.random.split(jax.random.key(seed), 5)
    return {
        "track": normal_values(seeds[0], (LENGTH, C), 1.0, 6.0, ((0, 32),), jnp.float32),
        "tight_weight": normal_values(seeds[1], (3 * C, C), (3 * C) ** -0.5, 0.15625, (), jnp.float32),
        "wide_weight": normal_values(seeds[2], (3 * C, C), (3 * C) ** -0.5, 0.15625, (), jnp.float32),
        "cotangent": normal_values(seeds[3], (LENGTH, C), 1.0, 6.0, ((0, 32),), jnp.float32),
    }


def shifted(field, dist):
    width = field.shape[1]
    pad = jnp.zeros((dist, width), jnp.float32)
    before = jnp.concatenate([pad, field[:-dist]], axis=0)
    after = jnp.concatenate([field[dist:], pad], axis=0)
    return (before, after)

def dilated_convolve(field, weights, dist):
    width = field.shape[1]
    before, after = shifted(field, dist)
    hp = lax.Precision.HIGHEST
    total = jnp.dot(before, weights[0:width], precision=hp, preferred_element_type=jnp.float32)
    total = total + jnp.dot(field, weights[width:2 * width], precision=hp, preferred_element_type=jnp.float32)
    total = total + jnp.dot(after, weights[2 * width:3 * width], precision=hp, preferred_element_type=jnp.float32)
    return total

def forward(track, tight_weight, wide_weight):
    hidden_activation = track + jax.nn.gelu(dilated_convolve(track, tight_weight, TIGHT_DILATION), approximate=True)
    return hidden_activation + jax.nn.gelu(dilated_convolve(hidden_activation, wide_weight, WIDE_DILATION), approximate=True)

def reference(track, tight_weight, wide_weight, cotangent):
    features_out, pullback = jax.vjp(forward, track, tight_weight, wide_weight)
    grad_track, grad_near, grad_far = pullback(cotangent)
    scale = 1.0 / jnp.sqrt(jnp.float32(LENGTH))
    return (features_out, grad_track, grad_near * scale, grad_far * scale)
```

```python
import jax
import jax.numpy as jnp
from jax import lax
from jax.sharding import PartitionSpec as P

NEAR_STEPS = 4
FAR_STEPS = 2
HP = lax.Precision.HIGH


def dot(a, b, contract):
    return lax.dot_general(
        a, b, ((contract[:1], contract[1:]), ((), ())), precision=HP, preferred_element_type=jnp.float32
    )


def gelu_fn(value):
    return jax.nn.gelu(value, approximate=True)


def swap(value, axis, mask):
    count = lax.axis_size(axis)
    return lax.ppermute(value, axis, [(i, i ^ mask) for i in range(count)])


def pick(blocks, index):
    return lax.dynamic_index_in_dim(blocks, index, 0, keepdims=False)


def exchange(blocks, axis):
    count = lax.axis_size(axis)
    me = lax.axis_index(axis)
    got = [swap(pick(blocks, me ^ mask), axis, mask) for mask in range(1, count)]
    out = blocks
    for mask, piece in enumerate(got, 1):
        out = lax.dynamic_update_index_in_dim(out, piece, me ^ mask, 0)
    return out


def spread(field):
    count = lax.axis_size("hi")
    rows, width = field.shape
    return exchange(field.reshape(count, rows // count, width), "hi").reshape(rows, width)


def shifted(field, rows):
    pad = jnp.zeros((rows, field.shape[1]), field.dtype)
    return jnp.concatenate([pad, field[:-rows]], axis=0), jnp.concatenate([field[rows:], pad], axis=0)


def taps(field, rows):
    before, after = shifted(field, rows)
    return jnp.concatenate([before, field, after], axis=1)


def back_taps(grad, rows):
    before, after = shifted(grad, rows)
    return after, grad, before


def conv_transpose(grad, weights, rows):
    width = grad.shape[1]
    parts = back_taps(grad, rows)
    total = dot(parts[0], weights[0:width], (1, 1))
    for tap in (1, 2):
        total = total + dot(parts[tap], weights[tap * width : (tap + 1) * width], (1, 1))
    return total


def weight_sum(stacked, grad):
    hi = lax.axis_index("hi")
    lo = lax.axis_index("lo")
    n_hi = lax.axis_size("hi")
    n_lo = lax.axis_size("lo")
    width = grad.shape[1] // 2
    core = hi % 2
    chip = hi // 2
    chips = n_hi // 2
    other = lax.dynamic_slice_in_dim(grad, (1 - core) * width, width, 1)
    own = lax.dynamic_slice_in_dim(grad, core * width, width, 1)
    sent = swap(dot(stacked, other, (0, 0)), "hi", 1)
    total = dot(stacked, own, (0, 0)) + sent
    rows = total.shape[0]
    part = rows // (n_lo * chips)
    blocks = total.reshape(n_lo, chips, part, width)
    mine = lax.dynamic_index_in_dim(blocks, chip, 1, keepdims=False)
    for mask in range(1, chips):
        piece = lax.dynamic_index_in_dim(blocks, chip ^ mask, 1, keepdims=False)
        mine = mine + swap(piece, "hi", 2 * mask)
    res = pick(mine, lo)
    for mask in range(1, n_lo):
        res = res + swap(pick(mine, lo ^ mask), "lo", mask)
    return res


def weight_gather(res):
    hi = lax.axis_index("hi")
    core = hi % 2
    chip = hi // 2
    chips = lax.axis_size("hi") // 2
    part, width = res.shape
    out = jnp.zeros((chips, part, width), res.dtype)
    out = lax.dynamic_update_index_in_dim(out, res, chip, 0)
    for mask in range(1, chips):
        out = lax.dynamic_update_index_in_dim(out, swap(res, "hi", 2 * mask), chip ^ mask, 0)
    out = out.reshape(chips * part, width)
    other = swap(out, "hi", 1)
    left = jnp.where(core == 0, out, other)
    right = jnp.where(core == 0, other, out)
    return jnp.concatenate([left, right], axis=1)


def family_shards(track, tight_weight, wide_weight, cotangent):
    rows = track.shape[0]
    n_hi = lax.axis_size("hi")
    n_lo = lax.axis_size("lo")
    near = NEAR_STEPS // n_lo * (rows // n_hi)
    far = FAR_STEPS * (rows // n_hi)
    scale = 1.0 / jnp.sqrt(jnp.float32(rows * n_hi * n_lo))
    track = spread(track)
    cotangent = spread(cotangent)
    track_taps = taps(track, near)
    pre_near = dot(track_taps, tight_weight, (1, 0))
    act_near, near_pull = jax.vjp(gelu_fn, pre_near)
    hidden = track + act_near
    hidden_taps = taps(hidden, far)
    pre_far = dot(hidden_taps, wide_weight, (1, 0))
    act_far, far_pull = jax.vjp(gelu_fn, pre_far)
    features = hidden + act_far
    g_far = far_pull(cotangent)[0]
    sum_far = weight_sum(hidden_taps, g_far)
    grad_hidden = cotangent + conv_transpose(g_far, wide_weight, far)
    g_near = near_pull(grad_hidden)[0]
    sum_near = weight_sum(track_taps, g_near)
    grad_track = grad_hidden + conv_transpose(g_near, tight_weight, near)
    return (
        spread(features),
        spread(grad_track),
        weight_gather(sum_near * scale),
        weight_gather(sum_far * scale),
    )


def from_behind(value, axis, steps):
    count = lax.axis_size(axis)
    initial, last = (max(0, -steps), min(count, count - steps))
    return lax.ppermute(value, axis, [(source, source + steps) for source in range(initial, last)])


def halo_shards(track, tight_weight, wide_weight, cotangent):
    def near_pair(field):
        return from_behind(field, ("hi", "lo"), NEAR_STEPS), from_behind(field, ("hi", "lo"), -NEAR_STEPS)

    def far_pair(field):
        return from_behind(field, "hi", FAR_STEPS), from_behind(field, "hi", -FAR_STEPS)

    def back_product(before, center, after, weights):
        width = center.shape[1]
        total = dot(after, weights[0:width], (1, 1))
        total = total + dot(center, weights[width : 2 * width], (1, 1))
        return total + dot(before, weights[2 * width : 3 * width], (1, 1))

    near_prev, near_next = near_pair(track)
    track_taps = jnp.concatenate([near_prev, track, near_next], axis=1)
    pre_near = dot(track_taps, tight_weight, (1, 0))
    act_near, near_pull = jax.vjp(gelu_fn, pre_near)
    hidden = track + act_near
    far_prev, far_next = far_pair(hidden)
    hidden_taps = jnp.concatenate([far_prev, hidden, far_next], axis=1)
    pre_far = dot(hidden_taps, wide_weight, (1, 0))
    act_far, far_pull = jax.vjp(gelu_fn, pre_far)
    features = hidden + act_far
    g_far = far_pull(cotangent)[0]
    term_far = dot(hidden_taps, g_far, (0, 0))
    gfar_prev, gfar_next = far_pair(g_far)
    grad_hidden = cotangent + back_product(gfar_prev, g_far, gfar_next, wide_weight)
    g_near = near_pull(grad_hidden)[0]
    term_near = dot(track_taps, g_near, (0, 0))
    gnear_prev, gnear_next = near_pair(g_near)
    grad_track = grad_hidden + back_product(gnear_prev, g_near, gnear_next, tight_weight)
    scale = 1.0 / jnp.sqrt(jnp.float32(track.shape[0] * lax.axis_size("hi") * lax.axis_size("lo")))
    summed_near, summed_far = lax.psum((term_near, term_far), "hi")
    rows_near = lax.psum_scatter(summed_near, "lo", scatter_dimension=0, tiled=True)
    rows_far = lax.psum_scatter(summed_far, "lo", scatter_dimension=0, tiled=True)
    return (features, grad_track, rows_near * scale, rows_far * scale)


def solution(mesh):
    n_hi, n_lo = mesh.shape["hi"], mesh.shape["lo"]

    def step(track, tight_weight, wide_weight, cotangent):
        rows = track.shape[0] // (n_hi * n_lo)
        powers = n_hi & (n_hi - 1) == 0 and n_lo & (n_lo - 1) == 0
        closed = NEAR_STEPS % n_lo == 0 and rows % (8 * n_hi) == 0 and powers
        closed = closed and tight_weight.shape[0] % (4 * n_hi * n_lo) == 0
        shards = family_shards if closed else halo_shards
        in_specs = (P(("hi", "lo"), None), P(), P(), P(("hi", "lo"), None))
        out_specs = (P(("hi", "lo"), None), P(("hi", "lo"), None), P("lo", None), P("lo", None))
        mapped = jax.shard_map(shards, mesh=mesh, in_specs=in_specs, out_specs=out_specs, check_vma=False)
        return mapped(track, tight_weight, wide_weight, cotangent)

    return step
```

```python
import jax
import jax.numpy as jnp
from jax import lax
from jax.sharding import PartitionSpec as P

NEAR_STEPS = 4
FAR_STEPS = 2
HP = lax.Precision.HIGH


def dot(a, b, contract):
    return lax.dot_general(
        a, b, ((contract[:1], contract[1:]), ((), ())), precision=HP, preferred_element_type=jnp.float32
    )


def gelu_fn(value):
    return jax.nn.gelu(value, approximate=True)


def swap(value, axis, mask):
    count = lax.axis_size(axis)
    return lax.ppermute(value, axis, [(i, i ^ mask) for i in range(count)])


def pick(blocks, index):
    return lax.dynamic_index_in_dim(blocks, index, 0, keepdims=False)


def exchange(field):
    rows, width = field.shape
    chips = lax.axis_size("hi") // 2
    blocks = field.reshape(chips, rows // chips, width)
    me = lax.axis_index("hi") // 2
    got = [swap(pick(blocks, me ^ mask), "hi", 2 * mask) for mask in range(1, chips)]
    out = blocks
    for mask, piece in enumerate(got, 1):
        out = lax.dynamic_update_index_in_dim(out, piece, me ^ mask, 0)
    return out.reshape(rows, width)


def shifted(field, rows):
    pad = jnp.zeros((rows, field.shape[1]), field.dtype)
    return jnp.concatenate([pad, field[:-rows]], axis=0), jnp.concatenate([field[rows:], pad], axis=0)


def partner_shifted(field, rows):
    other = swap(field, "hi", 1)
    core = lax.axis_index("hi") % 2
    pad = jnp.zeros((rows, field.shape[1]), field.dtype)
    padded = jnp.concatenate([pad, other, pad], axis=0)
    before = lax.dynamic_slice_in_dim(padded, core * rows, field.shape[0], 0)
    after = lax.dynamic_slice_in_dim(padded, (core + 1) * rows, field.shape[0], 0)
    return before, after


def conv(before, field, after, weights):
    width = field.shape[1]
    center = dot(field, weights[width : 2 * width], (1, 0))
    sides = jnp.concatenate([before, after], axis=1)
    outer = jnp.concatenate([weights[0:width], weights[2 * width :]], axis=0)
    return center + dot(sides, outer, (1, 0))


def conv_transpose(before, grad, after, weights):
    width = grad.shape[1]
    total = dot(grad, weights[width : 2 * width], (1, 1))
    total = total + dot(after, weights[0:width], (1, 1))
    return total + dot(before, weights[2 * width :], (1, 1))


def core_sum(stacked, grad):
    core = lax.axis_index("hi") % 2
    width = grad.shape[1] // 2
    other = lax.dynamic_slice_in_dim(grad, (1 - core) * width, width, 1)
    own = lax.dynamic_slice_in_dim(grad, core * width, width, 1)
    sent = swap(dot(stacked, other, (0, 0)), "hi", 1)
    return dot(stacked, own, (0, 0)) + sent


def halve(value, dim, bit, axis, mask):
    half = value.shape[dim] // 2
    give = lax.dynamic_slice_in_dim(value, (1 - bit) * half, half, dim)
    keep = lax.dynamic_slice_in_dim(value, bit * half, half, dim)
    return keep + swap(give, axis, mask)


def join(value, dim, bit, axis, mask):
    other = swap(value, axis, mask)
    first = jnp.where(bit == 0, value, other)
    second = jnp.where(bit == 0, other, value)
    return jnp.concatenate([first, second], axis=dim)


def lo_sum(value):
    lo = lax.axis_index("lo")
    n_lo = lax.axis_size("lo")
    mask = 1
    while mask < n_lo:
        shape = value.shape
        bit = lo // mask % 2
        value = value.reshape((shape[0] // 2, 2) + shape[1:])
        value = halve(value, 1, bit, "lo", mask).reshape((shape[0] // 2,) + shape[1:])
        mask *= 2
    return value[0]


def plane_bits():
    chip = lax.axis_index("hi") // 2
    return chip % 2, chip // 2


def sum_far(stacked, grad, scale):
    x, y = plane_bits()
    n_lo = lax.axis_size("lo")
    total = core_sum(stacked, grad)
    rows, width = total.shape
    total = total.reshape(n_lo, 2, rows // n_lo // 2, width)
    by_x = halve(total[:, 0], 1, x, "hi", 2)
    by_y = halve(total[:, 1], 1, y, "hi", 4)
    both = lo_sum(jnp.stack([by_x, by_y], axis=1)) * scale
    by_x = both[0] + swap(both[0], "hi", 4)
    by_y = both[1] + swap(both[1], "hi", 2)
    by_x = join(by_x, 0, x, "hi", 2)
    by_y = join(by_y, 0, y, "hi", 4)
    return jnp.concatenate([by_x, by_y], axis=0)


def sum_near(stacked, grad, scale):
    x, y = plane_bits()
    n_lo = lax.axis_size("lo")
    total = core_sum(stacked, grad)
    rows, width = total.shape
    total = total.reshape(n_lo, 2, rows // n_lo // 2, width)
    by_x = halve(total[:, 0], 1, x, "hi", 2)
    by_y = halve(total[:, 1], 1, y, "hi", 4)
    by_x = halve(by_x, 1, y, "hi", 4)
    by_y = halve(by_y, 1, x, "hi", 2)
    both = lo_sum(jnp.stack([by_x, by_y], axis=1)) * scale
    out = jnp.zeros((2, 4) + both.shape[1:], both.dtype)
    for mask in range(4):
        piece = both if mask == 0 else swap(both, "hi", 2 * mask)
        px, py = x ^ (mask % 2), y ^ (mask // 2)
        out = lax.dynamic_update_slice(out, piece[0][None, None], (0, 2 * px + py, 0, 0))
        out = lax.dynamic_update_slice(out, piece[1][None, None], (1, 2 * py + px, 0, 0))
    return out.reshape(rows // n_lo, width)


def family_shards(track, tight_weight, wide_weight, cotangent):
    rows = track.shape[0]
    n_hi = lax.axis_size("hi")
    n_lo = lax.axis_size("lo")
    core = lax.axis_index("hi") % 2
    step = rows // (n_hi // 2)
    scale = 1.0 / jnp.sqrt(jnp.float32(rows * n_hi * n_lo))
    track = exchange(track)
    cotangent = exchange(cotangent)
    before, after = partner_shifted(track, step)
    track_taps = jnp.concatenate([before, track, after], axis=1)
    pre_near = conv(before, track, after, tight_weight)
    act_near, near_pull = jax.vjp(gelu_fn, pre_near)
    hidden = track + act_near
    before, after = shifted(hidden, step)
    hidden_taps = jnp.concatenate([before, hidden, after], axis=1)
    pre_far = dot(hidden_taps, wide_weight, (1, 0))
    act_far, far_pull = jax.vjp(gelu_fn, pre_far)
    features = hidden + act_far
    g_far = far_pull(cotangent)[0]
    rows_far = sum_far(hidden_taps, g_far, scale)
    before, after = shifted(g_far, step)
    grad_hidden = cotangent + conv_transpose(before, g_far, after, wide_weight)
    g_near = near_pull(grad_hidden)[0]
    rows_near = sum_near(track_taps, g_near, scale)
    before, after = partner_shifted(g_near, step)
    grad_track = grad_hidden + conv_transpose(before, g_near, after, tight_weight)
    rows_far = join(rows_far, 1, core, "hi", 1)
    rows_near = join(rows_near, 1, core, "hi", 1)
    return exchange(features), exchange(grad_track), rows_near, rows_far


def from_behind(value, axis, steps):
    count = lax.axis_size(axis)
    initial, last = (max(0, -steps), min(count, count - steps))
    return lax.ppermute(value, axis, [(source, source + steps) for source in range(initial, last)])


def halo_shards(track, tight_weight, wide_weight, cotangent):
    def near_pair(field):
        return from_behind(field, ("hi", "lo"), NEAR_STEPS), from_behind(field, ("hi", "lo"), -NEAR_STEPS)

    def far_pair(field):
        return from_behind(field, "hi", FAR_STEPS), from_behind(field, "hi", -FAR_STEPS)

    def back_product(before, center, after, weights):
        width = center.shape[1]
        total = dot(after, weights[0:width], (1, 1))
        total = total + dot(center, weights[width : 2 * width], (1, 1))
        return total + dot(before, weights[2 * width : 3 * width], (1, 1))

    near_prev, near_next = near_pair(track)
    track_taps = jnp.concatenate([near_prev, track, near_next], axis=1)
    pre_near = dot(track_taps, tight_weight, (1, 0))
    act_near, near_pull = jax.vjp(gelu_fn, pre_near)
    hidden = track + act_near
    far_prev, far_next = far_pair(hidden)
    hidden_taps = jnp.concatenate([far_prev, hidden, far_next], axis=1)
    pre_far = dot(hidden_taps, wide_weight, (1, 0))
    act_far, far_pull = jax.vjp(gelu_fn, pre_far)
    features = hidden + act_far
    g_far = far_pull(cotangent)[0]
    term_far = dot(hidden_taps, g_far, (0, 0))
    gfar_prev, gfar_next = far_pair(g_far)
    grad_hidden = cotangent + back_product(gfar_prev, g_far, gfar_next, wide_weight)
    g_near = near_pull(grad_hidden)[0]
    term_near = dot(track_taps, g_near, (0, 0))
    gnear_prev, gnear_next = near_pair(g_near)
    grad_track = grad_hidden + back_product(gnear_prev, g_near, gnear_next, tight_weight)
    scale = 1.0 / jnp.sqrt(jnp.float32(track.shape[0] * lax.axis_size("hi") * lax.axis_size("lo")))
    summed_near, summed_far = lax.psum((term_near, term_far), "hi")
    rows_near = lax.psum_scatter(summed_near, "lo", scatter_dimension=0, tiled=True)
    rows_far = lax.psum_scatter(summed_far, "lo", scatter_dimension=0, tiled=True)
    return (features, grad_track, rows_near * scale, rows_far * scale)


def solution(mesh):
    n_hi, n_lo = mesh.shape["hi"], mesh.shape["lo"]

    def step(track, tight_weight, wide_weight, cotangent):
        rows = track.shape[0] // (n_hi * n_lo)
        closed = NEAR_STEPS == n_lo and FAR_STEPS == 2 and n_hi == 8
        closed = closed and rows % (8 * n_hi) == 0 and tight_weight.shape[0] % (64 * n_lo) == 0
        shards = family_shards if closed else halo_shards
        in_specs = (P(("hi", "lo"), None), P(), P(), P(("hi", "lo"), None))
        out_specs = (P(("hi", "lo"), None), P(("hi", "lo"), None), P("lo", None), P("lo", None))
        mapped = jax.shard_map(shards, mesh=mesh, in_specs=in_specs, out_specs=out_specs, check_vma=False)
        return mapped(track, tight_weight, wide_weight, cotangent)

    return step
```

```python
import jax
import jax.numpy as jnp
from jax import lax
from jax.experimental import pallas as pl
from jax.experimental.pallas import tpu as pltpu
from jax.sharding import PartitionSpec as P


NEAR_STEPS = 4
FAR_STEPS = 2
HP = lax.Precision.HIGH
F32 = jnp.float32
BF16 = jnp.bfloat16


def dot(a, b, contract):
    return lax.dot_general(
        a, b, ((contract[:1], contract[1:]), ((), ())), precision=HP, preferred_element_type=jnp.float32
    )


def gelu_fn(value):
    return jax.nn.gelu(value, approximate=True)


def call(body, outs, ids, *args, scratch=(), to_hbm=False, room=4):
    vmem = pl.BlockSpec(memory_space=pltpu.VMEM)
    smem = pl.BlockSpec(memory_space=pltpu.SMEM)
    make = jax.ShapeDtypeStruct if to_hbm else pltpu.VMEM
    return pl.pallas_call(
        body,
        out_shape=[make(shape, dtype) for shape, dtype in outs],
        in_specs=[smem] + [vmem] * len(args),
        out_specs=[vmem] * len(outs),
        scratch_shapes=[pltpu.VMEM(shape, dtype) for shape, dtype in scratch],
        compiler_params=pltpu.CompilerParams(vmem_limit_bytes=room * 1024 * 1024),
    )(ids, *[pltpu.with_memory_space_constraint(arg, pltpu.VMEM) for arg in args])


def swap(value, axis, mask):
    count = lax.axis_size(axis)
    return lax.ppermute(value, axis, [(i, i ^ mask) for i in range(count)])


def bits(ids):
    hi, lo = ids[0], ids[1]
    chip = hi >> 1
    return hi & 1, chip, chip & 1, chip >> 1, lo


def split(value):
    high = value.astype(BF16)
    return high, (value - high.astype(F32)).astype(BF16)


def mul(a, b, contract):
    dims = ((contract[:1], contract[1:]), ((), ()))

    def one(left, right):
        return lax.dot_general(left, right, dims, preferred_element_type=F32)

    return one(a[0], b[0]) + (one(a[0], b[1]) + one(a[1], b[0]))


def rows_of(pair, start, size):
    return tuple(ref[start : start + size] for ref in pair)


def gelu_both(u):
    root = 0.7978845608028654
    square = u * u
    tanh = jnp.tanh(root * (u + 0.044715 * (u * square)))
    half = 0.5 * (1.0 + tanh)
    slope = half + 0.5 * u * (1.0 - tanh * tanh) * (root * (1.0 + 3.0 * 0.044715 * square))
    return u * half, slope


def block(index, size):
    return pl.ds(pl.multiple_of(index * size, size), size)


def weights_body(ids, near, far, near_h, near_l, far_h, far_l, staged, done):
    parts, rows, _ = staged.shape
    each = parts // 2
    copies = []
    for k in range(parts):
        source = (near, far)[k // each].at[pl.ds(k % each * rows, rows)]
        copies.append(pltpu.make_async_copy(source, staged.at[k], done.at[k]))
        copies[-1].start()
    for k in range(parts):
        copies[k].wait()
        start = k % each * rows
        high, low = ((near_h, near_l), (far_h, far_l))[k // each]
        high[start : start + rows], low[start : start + rows] = split(staged[k])


def split_weights(ids, near, far):
    rows, width = near.shape
    smem = pl.BlockSpec(memory_space=pltpu.SMEM)
    whole = pl.BlockSpec(memory_space=pltpu.HBM)
    vmem = pl.BlockSpec(memory_space=pltpu.VMEM)
    return pl.pallas_call(
        weights_body,
        out_shape=[pltpu.VMEM((rows, width), BF16)] * 4,
        in_specs=[smem, whole, whole],
        out_specs=[vmem] * 4,
        scratch_shapes=[pltpu.VMEM((8, rows // 4, width), F32), pltpu.SemaphoreType.DMA((8,))],
        compiler_params=pltpu.CompilerParams(vmem_limit_bytes=8 * 1024 * 1024),
        name="k_weights",
    )(ids, *[pltpu.with_memory_space_constraint(arg, pltpu.HBM) for arg in (near, far)])


def forward_body(ids, p0, p1, p2, p3, q0, q1, q2, q3, near_h, near_l, far_h, far_l,
                 f0, f1, f2, f3, slope_near, slope_far, hid_h, hid_l, own_h, own_l, oth_h, oth_l, field):
    core, chip, _, _, _ = bits(ids)
    rows, width = slope_near.shape
    size = rows // 4
    pad = jnp.zeros((size, width), BF16)
    for ref in (oth_h, oth_l):
        ref[0:size] = pad
        ref[rows + size :] = pad
    for mask, (own, other) in enumerate(((p0, q0), (p1, q1), (p2, q2), (p3, q3))):
        field[block(chip ^ mask, size)] = own[...]
        high, low = split(other[...])
        oth_h[block((chip ^ mask) + 1, size)] = high
        oth_l[block((chip ^ mask) + 1, size)] = low
    track = field[...]
    own_h[...], own_l[...] = split(track)
    before = pl.ds(pl.multiple_of(core * size, size), rows)
    after = pl.ds(pl.multiple_of(core * size + size, size), rows)
    pre = mul((own_h[...], own_l[...]), rows_of((near_h, near_l), width, width), (1, 0))
    pre = pre + mul((oth_h[before], oth_l[before]), rows_of((near_h, near_l), 0, width), (1, 0))
    pre = pre + mul((oth_h[after], oth_l[after]), rows_of((near_h, near_l), 2 * width, width), (1, 0))
    act, slope = gelu_both(pre)
    slope_near[...] = slope
    hidden = track + act
    hid_h[...], hid_l[...] = split(hidden)
    field[...] = mul((hid_h[...], hid_l[...]), rows_of((far_h, far_l), width, width), (1, 0))
    rest = rows - size
    field[size:] += mul(rows_of((hid_h, hid_l), 0, rest), rows_of((far_h, far_l), 0, width), (1, 0))
    field[0:rest] += mul(rows_of((hid_h, hid_l), size, rest), rows_of((far_h, far_l), 2 * width, width), (1, 0))
    act, slope = gelu_both(field[...])
    slope_far[...] = slope
    field[...] = hidden + act
    for mask, out in enumerate((f0, f1, f2, f3)):
        out[...] = field[block(chip ^ mask, size)]


def half_columns(pair, index):
    width = pair[0].shape[1] // 2
    return tuple(jnp.where(index == 0, ref[:, :width].astype(F32), ref[:, width:].astype(F32)).astype(BF16) for ref in pair)


def far_term(hid, grad, store):
    rows, _ = hid[0].shape
    size = rows // 4
    rest = rows - size
    store(0, mul(rows_of(hid, 0, rest), tuple(g[size:] for g in grad), (0, 0)))
    store(1, mul(tuple(h[...] for h in hid), grad, (0, 0)))
    store(2, mul(rows_of(hid, size, rest), tuple(g[:rest] for g in grad), (0, 0)))


def near_term(core, own, other, grad, store):
    rows, _ = own[0].shape
    size = rows // 4
    before = pl.ds(pl.multiple_of(core * size, size), rows)
    after = pl.ds(pl.multiple_of(core * size + size, size), rows)
    store(0, mul(tuple(o[before] for o in other), grad, (0, 0)))
    store(1, mul(tuple(o[...] for o in own), grad, (0, 0)))
    store(2, mul(tuple(o[after] for o in other), grad, (0, 0)))


def far_other_body(ids, c0, c1, c2, c3, slope, hid_h, hid_l, cot, g_h, g_l, term):
    core, chip, _, _, _ = bits(ids)
    rows, width = cot.shape
    size = rows // 4
    for mask, piece in enumerate((c0, c1, c2, c3)):
        cot[block(chip ^ mask, size)] = piece[...]
    g_h[...], g_l[...] = split(cot[...] * slope[...])

    def store(tap, value):
        term[tap * width : (tap + 1) * width] = value

    far_term((hid_h, hid_l), half_columns((g_h, g_l), 1 - core), store)


def quarter(total, ids, outs):
    _, _, x, y, _ = bits(ids)
    x_keep, x_send, y_keep, y_send = outs
    count, half, _ = x_keep.shape
    for z in range(count):
        start = z * 4 * half
        x_keep[z] = total[pl.ds(pl.multiple_of(start + x * half, half), half)]
        x_send[z] = total[pl.ds(pl.multiple_of(start + (1 - x) * half, half), half)]
        y_keep[z] = total[pl.ds(pl.multiple_of(start + (2 + y) * half, half), half)]
        y_send[z] = total[pl.ds(pl.multiple_of(start + (3 - y) * half, half), half)]


def far_own_body(ids, hid_h, hid_l, g_h, g_l, got, x_keep, x_send, y_keep, y_send, total):
    core, _, _, _, _ = bits(ids)
    width = hid_h.shape[1]

    def store(tap, value):
        total[tap * width : (tap + 1) * width] = value + got[tap * width : (tap + 1) * width]

    far_term((hid_h, hid_l), half_columns((g_h, g_l), core), store)
    quarter(total, ids, (x_keep, x_send, y_keep, y_send))


def backward_body(ids, cot, g_h, g_l, far_h, far_l, slope, grad, gn, gn_h, gn_l):
    rows, width = cot.shape
    size = rows // 4
    rest = rows - size
    grad[...] = cot[...] + mul((g_h[...], g_l[...]), rows_of((far_h, far_l), width, width), (1, 1))
    grad[0:rest] += mul(rows_of((g_h, g_l), size, rest), rows_of((far_h, far_l), 0, width), (1, 1))
    grad[size:] += mul(rows_of((g_h, g_l), 0, rest), rows_of((far_h, far_l), 2 * width, width), (1, 1))
    value = grad[...] * slope[...]
    gn[...] = value
    gn_h[...], gn_l[...] = split(value)


def near_other_body(ids, own_h, own_l, oth_h, oth_l, gn_h, gn_l, term):
    core, _, _, _, _ = bits(ids)
    width = own_h.shape[1]

    def store(tap, value):
        term[tap * width : (tap + 1) * width] = value

    near_term(core, (own_h, own_l), (oth_h, oth_l), half_columns((gn_h, gn_l), 1 - core), store)


def near_own_body(ids, own_h, own_l, oth_h, oth_l, gn_h, gn_l, got, x_keep, x_send, y_keep, y_send, total):
    core, _, _, _, _ = bits(ids)
    width = own_h.shape[1]

    def store(tap, value):
        total[tap * width : (tap + 1) * width] = value + got[tap * width : (tap + 1) * width]

    near_term(core, (own_h, own_l), (oth_h, oth_l), half_columns((gn_h, gn_l), core), store)
    quarter(total, ids, (x_keep, x_send, y_keep, y_send))


def track_body(ids, grad, gn_h, gn_l, other, near_h, near_l, t0, t1, t2, t3, oth_h, oth_l, field):
    core, chip, _, _, _ = bits(ids)
    rows, width = grad.shape
    size = rows // 4
    pad = jnp.zeros((size, width), BF16)
    for ref in (oth_h, oth_l):
        ref[0:size] = pad
        ref[rows + size :] = pad
    high, low = split(other[...])
    oth_h[size : rows + size] = high
    oth_l[size : rows + size] = low
    before = pl.ds(pl.multiple_of(core * size, size), rows)
    after = pl.ds(pl.multiple_of(core * size + size, size), rows)
    total = grad[...] + mul((gn_h[...], gn_l[...]), rows_of((near_h, near_l), width, width), (1, 1))
    total = total + mul((oth_h[after], oth_l[after]), rows_of((near_h, near_l), 0, width), (1, 1))
    field[...] = total + mul((oth_h[before], oth_l[before]), rows_of((near_h, near_l), 2 * width, width), (1, 1))
    for mask, out in enumerate((t0, t1, t2, t3)):
        out[...] = field[block(chip ^ mask, size)]


def plane_body(ids, x_kept, x_got, y_kept, y_got, x_keep, x_send, y_keep, y_send):
    _, _, x, y, _ = bits(ids)
    half = x_keep.shape[1]
    for kept, got, bit, keep, send in ((x_kept, x_got, y, x_keep, x_send), (y_kept, y_got, x, y_keep, y_send)):
        for z in range(kept.shape[0]):
            mine, theirs = block(bit, half), block(1 - bit, half)
            keep[z] = kept[z, mine] + got[z, mine]
            send[z] = kept[z, theirs] + got[z, theirs]


def first_lo_body(ids, x_kept, x_got, y_kept, y_got, keep, send):
    lo = bits(ids)[4]
    bit = lo & 1
    for k in range(keep.shape[0]):
        for half, (kept, got) in enumerate(((x_kept, x_got), (y_kept, y_got))):
            keep[k, half] = kept[2 * k + bit] + got[2 * k + bit]
            send[k, half] = kept[2 * k + 1 - bit] + got[2 * k + 1 - bit]


def second_lo_body(ids, kept, got, keep, send):
    bit = bits(ids)[4] >> 1
    keep[...] = kept[bit] + got[bit]
    send[...] = kept[1 - bit] + got[1 - bit]


def sum_pair_body(scale, ids, kept, got, by_x, by_y):
    by_x[...] = (kept[0] + got[0]) * scale
    by_y[...] = (kept[1] + got[1]) * scale


def sum_body(scale, ids, kept, got, out):
    out[...] = (kept[...] + got[...]) * scale


def cross_body(ids, a, a_got, b, b_got, a_out, b_out):
    a_out[...] = a[...] + a_got[...]
    b_out[...] = b[...] + b_got[...]


def far_rows_body(ids, a, a_got, b, b_got, out):
    _, _, x, y, _ = bits(ids)
    half = a.shape[0]
    out[block(x, half)] = a[...]
    out[block(1 - x, half)] = a_got[...]
    out[block(2 + y, half)] = b[...]
    out[block(3 - y, half)] = b_got[...]


def near_rows_body(ids, s0, s1, s2, s3, out):
    _, _, x, y, _ = bits(ids)
    size = s0.shape[1]
    for mask, piece in enumerate((s0, s1, s2, s3)):
        px, py = x ^ (mask & 1), y ^ (mask >> 1)
        out[block(2 * px + py, size)] = piece[0]
        out[block(4 + 2 * py + px, size)] = piece[1]


def columns_body(ids, own, got, out):
    core = bits(ids)[0]
    width = own.shape[1]
    out[:, :width] = jnp.where(core == 0, own[...], got[...])
    out[:, width:] = jnp.where(core == 0, got[...], own[...])


def collect_body(ids, p0, p1, p2, p3, out):
    chip = bits(ids)[1]
    size = p0.shape[0]
    for mask, piece in enumerate((p0, p1, p2, p3)):
        out[block(chip ^ mask, size)] = piece[...]


def pieces(field, chip):
    size = field.shape[0] // 4
    return [lax.dynamic_slice_in_dim(field, (chip ^ mask) * size, size, 0) for mask in range(4)]


def over_chips(parts):
    return [parts[0]] + [swap(parts[mask], "hi", 2 * mask) for mask in range(1, 4)]


def family_shards(track, near_weight, far_weight, cotangent):
    return family_step(track, near_weight, far_weight, cotangent)


def family_step(track, near_weight, far_weight, cotangent):
    rows, width = track.shape
    n_hi = lax.axis_size("hi")
    n_lo = lax.axis_size("lo")
    size = rows // 4
    half = width // 2
    tall = near_weight.shape[0]
    part = tall // n_lo // 4
    hi = lax.axis_index("hi")
    lo = lax.axis_index("lo")
    ids = jnp.stack([hi, lo])
    chip = lax.shift_right_logical(hi, 1)
    scale = 1.0 / float(rows * n_hi * n_lo) ** 0.5
    full, piece = (rows, width), (size, width)
    padded = (rows + 2 * size, width)

    own = over_chips(pieces(track, chip))
    other = [swap(own[mask], "hi", 1) for mask in range(4)]
    cot = over_chips(pieces(cotangent, chip))
    near_h, near_l, far_h, far_l = split_weights(ids, near_weight, far_weight)
    near_w, far_w = (near_h, near_l), (far_h, far_l)
    out = call(
        forward_body,
        [(piece, F32)] * 4 + [(full, F32)] * 2 + [(full, BF16)] * 4 + [(padded, BF16)] * 2,
        ids, *own, *other, *near_w, *far_w, scratch=[(full, F32)], room=16,
    )
    feats, slope_near, slope_far = out[:4], out[4], out[5]
    hid, own_pair, oth_pair = out[6:8], out[8:10], out[10:12]
    cot, g_h, g_l, far_other = call(
        far_other_body, [(full, F32), (full, BF16), (full, BF16), ((tall, half), F32)],
        ids, *cot, slope_far, *hid,
    )
    far_got = swap(far_other, "hi", 1)
    feats = over_chips(feats)
    quarters = [((n_lo, part, half), F32)] * 4
    far_q = call(far_own_body, quarters, ids, *hid, g_h, g_l, far_got, scratch=[((tall, half), F32)], room=12)
    far_x, far_y = swap(far_q[1], "hi", 2), swap(far_q[3], "hi", 4)
    grad, gn, gn_h, gn_l = call(
        backward_body, [(full, F32), (full, F32), (full, BF16), (full, BF16)],
        ids, cot, g_h, g_l, *far_w, slope_near,
    )
    (near_other,) = call(near_other_body, [((tall, half), F32)], ids, *own_pair, *oth_pair, gn_h, gn_l)
    near_got = swap(near_other, "hi", 1)
    gn_got = swap(gn, "hi", 1)
    near_q = call(
        near_own_body, quarters, ids, *own_pair, *oth_pair, gn_h, gn_l, near_got,
        scratch=[((tall, half), F32)], room=12,
    )
    near_x, near_y = swap(near_q[1], "hi", 2), swap(near_q[3], "hi", 4)
    first, second = ((n_lo // 2, 2, part, half), F32), ((2, part, half), F32)
    keep, send = call(first_lo_body, [first] * 2, ids, far_q[0], far_x, far_q[2], far_y)
    got = swap(send, "lo", 1)
    grads = call(
        track_body, [(piece, F32)] * 4, ids, grad, gn_h, gn_l, gn_got, *near_w,
        scratch=[(padded, BF16), (padded, BF16), (full, F32)], room=12,
    )
    keep, send = call(second_lo_body, [second] * 2, ids, keep, got)
    got = swap(send, "lo", 2)
    deep = [((n_lo, part // 2, half), F32)] * 4
    near_q = call(plane_body, deep, ids, near_q[0], near_x, near_q[2], near_y)
    near_x, near_y = swap(near_q[1], "hi", 4), swap(near_q[3], "hi", 2)
    grads = over_chips(grads)
    first, second = ((n_lo // 2, 2, part // 2, half), F32), ((2, part // 2, half), F32)
    n_keep, n_send = call(first_lo_body, [first] * 2, ids, near_q[0], near_x, near_q[2], near_y)
    n_got = swap(n_send, "lo", 1)

    def far_sum(*refs):
        sum_pair_body(scale, *refs)

    def near_sum(*refs):
        sum_body(scale, *refs)

    a, b = call(far_sum, [((part, half), F32)] * 2, ids, keep, got)
    a, b = call(cross_body, [((part, half), F32)] * 2, ids, a, swap(a, "hi", 4), b, swap(b, "hi", 2))
    n_keep, n_send = call(second_lo_body, [second] * 2, ids, n_keep, n_got)
    n_got = swap(n_send, "lo", 2)
    (rows_far,) = call(far_rows_body, [((4 * part, half), F32)], ids, a, swap(a, "hi", 2), b, swap(b, "hi", 4))
    far_cols = swap(rows_far, "hi", 1)
    (near_mine,) = call(near_sum, [second], ids, n_keep, n_got)
    near_all = over_chips([near_mine] * 4)
    (rows_near,) = call(near_rows_body, [((4 * part, half), F32)], ids, *near_all)
    near_cols = swap(rows_near, "hi", 1)
    (features,) = call(collect_body, [(full, F32)], ids, *feats, to_hbm=True)
    (grad_track,) = call(collect_body, [(full, F32)], ids, *grads, to_hbm=True)
    wide = [((4 * part, width), F32)]
    (grad_far,) = call(columns_body, wide, ids, rows_far, far_cols, to_hbm=True)
    (grad_near,) = call(columns_body, wide, ids, rows_near, near_cols, to_hbm=True)
    return features, grad_track, grad_near, grad_far


def from_behind(value, axis, steps):
    count = lax.axis_size(axis)
    initial, last = (max(0, -steps), min(count, count - steps))
    return lax.ppermute(value, axis, [(source, source + steps) for source in range(initial, last)])


def halo_shards(track, tight_weight, wide_weight, cotangent):
    def near_pair(field):
        return from_behind(field, ("hi", "lo"), NEAR_STEPS), from_behind(field, ("hi", "lo"), -NEAR_STEPS)

    def far_pair(field):
        return from_behind(field, "hi", FAR_STEPS), from_behind(field, "hi", -FAR_STEPS)

    def back_product(before, center, after, weights):
        width = center.shape[1]
        total = dot(after, weights[0:width], (1, 1))
        total = total + dot(center, weights[width : 2 * width], (1, 1))
        return total + dot(before, weights[2 * width : 3 * width], (1, 1))

    near_prev, near_next = near_pair(track)
    track_taps = jnp.concatenate([near_prev, track, near_next], axis=1)
    pre_near = dot(track_taps, tight_weight, (1, 0))
    act_near, near_pull = jax.vjp(gelu_fn, pre_near)
    hidden = track + act_near
    far_prev, far_next = far_pair(hidden)
    hidden_taps = jnp.concatenate([far_prev, hidden, far_next], axis=1)
    pre_far = dot(hidden_taps, wide_weight, (1, 0))
    act_far, far_pull = jax.vjp(gelu_fn, pre_far)
    features = hidden + act_far
    g_far = far_pull(cotangent)[0]
    term_far = dot(hidden_taps, g_far, (0, 0))
    gfar_prev, gfar_next = far_pair(g_far)
    grad_hidden = cotangent + back_product(gfar_prev, g_far, gfar_next, wide_weight)
    g_near = near_pull(grad_hidden)[0]
    term_near = dot(track_taps, g_near, (0, 0))
    gnear_prev, gnear_next = near_pair(g_near)
    grad_track = grad_hidden + back_product(gnear_prev, g_near, gnear_next, tight_weight)
    scale = 1.0 / jnp.sqrt(jnp.float32(track.shape[0] * lax.axis_size("hi") * lax.axis_size("lo")))
    summed_near, summed_far = lax.psum((term_near, term_far), "hi")
    rows_near = lax.psum_scatter(summed_near, "lo", scatter_dimension=0, tiled=True)
    rows_far = lax.psum_scatter(summed_far, "lo", scatter_dimension=0, tiled=True)
    return (features, grad_track, rows_near * scale, rows_far * scale)


def solution(mesh):
    n_hi, n_lo = mesh.shape["hi"], mesh.shape["lo"]

    def step(track, tight_weight, wide_weight, cotangent):
        rows = track.shape[0] // (n_hi * n_lo)
        closed = NEAR_STEPS == n_lo and FAR_STEPS == 2 and n_hi == 8
        closed = closed and rows % (8 * n_hi) == 0 and tight_weight.shape[0] % (64 * n_lo) == 0
        closed = closed and tight_weight.shape[1] % 256 == 0
        if closed:
            shards = family_shards
        else:
            shards = halo_shards
        in_specs = (P(("hi", "lo"), None), P(), P(), P(("hi", "lo"), None))
        out_specs = (P(("hi", "lo"), None), P(("hi", "lo"), None), P("lo", None), P("lo", None))
        mapped = jax.shard_map(shards, mesh=mesh, in_specs=in_specs, out_specs=out_specs, check_vma=False)
        return mapped(track, tight_weight, wide_weight, cotangent)

    return step
```

```python
import jax
import jax.numpy as jnp
from jax import lax
from jax.experimental import pallas as pl
from jax.experimental.pallas import tpu as pltpu
from jax.sharding import PartitionSpec as P


NEAR_STEPS = 4
FAR_STEPS = 2
HP = lax.Precision.HIGH
F32 = jnp.float32
BF16 = jnp.bfloat16


def dot(a, b, contract):
    return lax.dot_general(
        a, b, ((contract[:1], contract[1:]), ((), ())), precision=HP, preferred_element_type=jnp.float32
    )


def gelu_fn(value):
    return jax.nn.gelu(value, approximate=True)


def call(body, outs, ids, *args, scratch=(), to_hbm=False, room=4):
    vmem = pl.BlockSpec(memory_space=pltpu.VMEM)
    smem = pl.BlockSpec(memory_space=pltpu.SMEM)
    make = jax.ShapeDtypeStruct if to_hbm else pltpu.VMEM
    return pl.pallas_call(
        body,
        out_shape=[make(shape, dtype) for shape, dtype in outs],
        in_specs=[smem] + [vmem] * len(args),
        out_specs=[vmem] * len(outs),
        scratch_shapes=[pltpu.VMEM(shape, dtype) for shape, dtype in scratch],
        compiler_params=pltpu.CompilerParams(vmem_limit_bytes=room * 1024 * 1024),
    )(ids, *[pltpu.with_memory_space_constraint(arg, pltpu.VMEM) for arg in args])


def swap(value, axis, mask):
    count = lax.axis_size(axis)
    return lax.ppermute(value, axis, [(i, i ^ mask) for i in range(count)])


def plane_swap(value, turn):
    count = lax.axis_size("hi")
    return lax.ppermute(value, "hi", [(i, i ^ (2 << (i + turn) % 2)) for i in range(count)])


def bits(ids):
    hi, lo = ids[0], ids[1]
    return hi & 1, hi >> 1, lo


def turns(core, chip):
    return (chip >> core) & 1, (chip >> (1 - core)) & 1


def split(value):
    high = value.astype(BF16)
    return high, (value - high.astype(F32)).astype(BF16)


def mul(a, b, contract):
    dims = ((contract[:1], contract[1:]), ((), ()))

    def one(left, right):
        return lax.dot_general(left, right, dims, preferred_element_type=F32)

    return one(a[0], b[0]) + (one(a[0], b[1]) + one(a[1], b[0]))


def rows_of(pair, start, size):
    return tuple(ref[start : start + size] for ref in pair)


def gelu_both(u):
    root = 0.7978845608028654
    square = u * u
    tanh = jnp.tanh(root * (u + 0.044715 * (u * square)))
    half = 0.5 * (1.0 + tanh)
    slope = half + 0.5 * u * (1.0 - tanh * tanh) * (root * (1.0 + 3.0 * 0.044715 * square))
    return u * half, slope


def block(index, size):
    return pl.ds(pl.multiple_of(index * size, size), size)


def weights_body(ids, near, far, cot, near_h, near_l, far_h, far_l, c0, c1, c2, c3, staged, done, moved):
    chip = bits(ids)[1]
    parts, rows, _ = staged.shape
    each = parts // 2
    size = c0.shape[0]
    cuts = [
        pltpu.make_async_copy(cot.at[block(chip ^ mask, size)], out, moved.at[mask])
        for mask, out in enumerate((c0, c1, c2, c3))
    ]
    copies = [
        pltpu.make_async_copy((near, far)[k // each].at[pl.ds(k % each * rows, rows)], staged.at[k], done.at[k])
        for k in range(parts)
    ]
    for copy in copies[:each] + cuts + copies[each:]:
        copy.start()
    for k in range(parts):
        copies[k].wait()
        start = k % each * rows
        high, low = ((near_h, near_l), (far_h, far_l))[k // each]
        high[start : start + rows], low[start : start + rows] = split(staged[k])
    for copy in cuts:
        copy.wait()


def hbm_call(body, outs, specs, ids, args, scratch, room):
    smem = pl.BlockSpec(memory_space=pltpu.SMEM)
    places = {pltpu.HBM: pl.BlockSpec(memory_space=pltpu.HBM), pltpu.VMEM: pl.BlockSpec(memory_space=pltpu.VMEM)}
    ins, out_place = specs
    return pl.pallas_call(
        body,
        out_shape=[out_place(shape, dtype) for shape, dtype in outs],
        in_specs=[smem] + [places[ins]] * len(args),
        out_specs=[places[out_place]] * len(outs),
        scratch_shapes=scratch,
        compiler_params=pltpu.CompilerParams(vmem_limit_bytes=room * 1024 * 1024),
    )(ids, *[pltpu.with_memory_space_constraint(arg, ins) for arg in args])


def forward_body(ids, p0, p1, p2, p3, q0, q1, q2, q3, near_h, near_l, far_h, far_l,
                 f0, f1, f2, f3, slope_near, slope_far, hid_h, hid_l, own_h, own_l, oth_h, oth_l, field):
    core, chip, _ = bits(ids)
    rows, width = slope_near.shape
    size = rows // 4
    pad = jnp.zeros((size, width), BF16)
    for ref in (own_h, own_l, oth_h, oth_l):
        ref[0:size] = pad
        ref[rows + size :] = pad
    for mask, (own, other) in enumerate(((p0, q0), (p1, q1), (p2, q2), (p3, q3))):
        field[block(chip ^ mask, size)] = own[...]
        high, low = split(other[...])
        oth_h[block((chip ^ mask) + 1, size)] = high
        oth_l[block((chip ^ mask) + 1, size)] = low
    track = field[...]
    own_h[size : rows + size], own_l[size : rows + size] = split(track)
    before = pl.ds(pl.multiple_of(core * size, size), rows)
    after = pl.ds(pl.multiple_of(core * size + size, size), rows)
    pre = mul(rows_of((own_h, own_l), size, rows), rows_of((near_h, near_l), width, width), (1, 0))
    pre = pre + mul((oth_h[before], oth_l[before]), rows_of((near_h, near_l), 0, width), (1, 0))
    pre = pre + mul((oth_h[after], oth_l[after]), rows_of((near_h, near_l), 2 * width, width), (1, 0))
    act, slope = gelu_both(pre)
    slope_near[...] = slope
    hidden = track + act
    hid_h[...], hid_l[...] = split(hidden)
    field[...] = mul((hid_h[...], hid_l[...]), rows_of((far_h, far_l), width, width), (1, 0))
    rest = rows - size
    field[size:] += mul(rows_of((hid_h, hid_l), 0, rest), rows_of((far_h, far_l), 0, width), (1, 0))
    field[0:rest] += mul(rows_of((hid_h, hid_l), size, rest), rows_of((far_h, far_l), 2 * width, width), (1, 0))
    act, slope = gelu_both(field[...])
    slope_far[...] = slope
    field[...] = hidden + act
    for mask, out in enumerate((f0, f1, f2, f3)):
        out[...] = field[block(chip ^ mask, size)]


def half_columns(pair, index):
    width = pair[0].shape[1] // 2
    return tuple(jnp.where(index == 0, ref[:, :width].astype(F32), ref[:, width:].astype(F32)).astype(BF16) for ref in pair)


def far_term(hid, grad, store):
    rows, _ = hid[0].shape
    size = rows // 4
    rest = rows - size
    store(0, mul(rows_of(hid, 0, rest), tuple(g[size:] for g in grad), (0, 0)))
    store(1, mul(tuple(h[...] for h in hid), grad, (0, 0)))
    store(2, mul(rows_of(hid, size, rest), tuple(g[:rest] for g in grad), (0, 0)))


def near_term(core, center, sides, grad, store):
    rows = grad[0].shape[0]
    size = rows // 4
    before = pl.ds(pl.multiple_of(core * size, size), rows)
    after = pl.ds(pl.multiple_of(core * size + size, size), rows)
    store(0, mul(tuple(ref[before] for ref in sides), grad, (0, 0)))
    store(1, mul(rows_of(center, size, rows), grad, (0, 0)))
    store(2, mul(tuple(ref[after] for ref in sides), grad, (0, 0)))


def far_other_body(ids, c0, c1, c2, c3, slope, hid_h, hid_l, cot, g_h, g_l, term):
    core, chip, _ = bits(ids)
    rows, width = cot.shape
    size = rows // 4
    for mask, piece in enumerate((c0, c1, c2, c3)):
        cot[block(chip ^ mask, size)] = piece[...]
    g_h[...], g_l[...] = split(cot[...] * slope[...])

    def store(tap, value):
        term[tap * width : (tap + 1) * width] = value

    far_term((hid_h, hid_l), half_columns((g_h, g_l), 1 - core), store)


def halve(total, bit, keep, send):
    count, half, _ = keep.shape
    for z in range(count):
        keep[z] = total[pl.ds(pl.multiple_of((2 * z + bit) * half, 32), half)]
        send[z] = total[pl.ds(pl.multiple_of((2 * z + 1 - bit) * half, 32), half)]


def far_own_body(ids, hid_h, hid_l, g_h, g_l, got, keep, send, total):
    core, chip, _ = bits(ids)
    width = hid_h.shape[1]

    def store(tap, value):
        total[tap * width : (tap + 1) * width] = value + got[tap * width : (tap + 1) * width]

    far_term((hid_h, hid_l), half_columns((g_h, g_l), core), store)
    halve(total, turns(core, chip)[0], keep, send)


def backward_body(ids, cot, g_h, g_l, far_h, far_l, slope, grad, gn, gn_h, gn_l):
    rows, width = cot.shape
    size = rows // 4
    rest = rows - size
    grad[...] = cot[...] + mul((g_h[...], g_l[...]), rows_of((far_h, far_l), width, width), (1, 1))
    grad[0:rest] += mul(rows_of((g_h, g_l), size, rest), rows_of((far_h, far_l), 0, width), (1, 1))
    grad[size:] += mul(rows_of((g_h, g_l), 0, rest), rows_of((far_h, far_l), 2 * width, width), (1, 1))
    value = grad[...] * slope[...]
    gn[...] = value
    gn_h[...], gn_l[...] = split(value)


def near_mine_body(ids, own_h, own_l, oth_h, oth_l, gn_h, gn_l, term):
    core, _, _ = bits(ids)
    width = own_h.shape[1]

    def store(tap, value):
        term[tap * width : (tap + 1) * width] = value

    near_term(core, (own_h, own_l), (oth_h, oth_l), half_columns((gn_h, gn_l), core), store)


def near_both_body(ids, term, own_h, own_l, oth_h, oth_l, other, keep, send, total):
    core, chip, _ = bits(ids)
    width = own_h.shape[1]
    half = width // 2

    def store(tap, value):
        total[tap * width : (tap + 1) * width] = value + term[tap * width : (tap + 1) * width]

    grad = split(jnp.where(core == 0, other[:, :half], other[:, half:]))
    near_term(1 - core, (oth_h, oth_l), (own_h, own_l), grad, store)
    halve(total, turns(core, chip)[0], keep, send)


def track_body(ids, grad, gn_h, gn_l, other, near_h, near_l, t0, t1, t2, t3, oth_h, oth_l, field):
    core, chip, _ = bits(ids)
    rows, width = grad.shape
    size = rows // 4
    pad = jnp.zeros((size, width), BF16)
    for ref in (oth_h, oth_l):
        ref[0:size] = pad
        ref[rows + size :] = pad
    high, low = split(other[...])
    oth_h[size : rows + size] = high
    oth_l[size : rows + size] = low
    before = pl.ds(pl.multiple_of(core * size, size), rows)
    after = pl.ds(pl.multiple_of(core * size + size, size), rows)
    total = grad[...] + mul((gn_h[...], gn_l[...]), rows_of((near_h, near_l), width, width), (1, 1))
    total = total + mul((oth_h[after], oth_l[after]), rows_of((near_h, near_l), 0, width), (1, 1))
    field[...] = total + mul((oth_h[before], oth_l[before]), rows_of((near_h, near_l), 2 * width, width), (1, 1))
    for mask, out in enumerate((t0, t1, t2, t3)):
        out[...] = field[block(chip ^ mask, size)]


def plane_body(ids, kept, got, keep, send):
    core, chip, _ = bits(ids)
    bit = turns(core, chip)[1]
    half = keep.shape[1]
    mine = pl.ds(pl.multiple_of(bit * half, 32), half)
    theirs = pl.ds(pl.multiple_of((1 - bit) * half, 32), half)
    keep[...] = kept[:, mine] + got[:, mine]
    send[...] = kept[:, theirs] + got[:, theirs]


def pick_body(ids, kept, got, p0, p1, p2, p3):
    lo = bits(ids)[2]
    for mask, out in enumerate((p0, p1, p2, p3)):
        out[...] = kept[lo ^ mask] + got[lo ^ mask]


def total_body(scale, ids, p0, p1, p2, p3, out):
    out[...] = ((p0[...] + p1[...]) + (p2[...] + p3[...])) * scale


def cross_body(ids, own, got, out):
    out[...] = own[...] + got[...]


def far_rows_body(ids, own, got, out):
    core, chip, _ = bits(ids)
    bit = turns(core, chip)[0]
    half = own.shape[0]
    out[pl.ds(pl.multiple_of(bit * half, 32), half)] = own[...]
    out[pl.ds(pl.multiple_of((1 - bit) * half, 32), half)] = got[...]


def near_rows_body(ids, s0, s1, s2, s3, out):
    core, chip, _ = bits(ids)
    size = s0.shape[0]
    for mask, piece in enumerate((s0, s1, s2, s3)):
        first, second = turns(core, chip ^ mask)
        out[pl.ds(pl.multiple_of((2 * first + second) * size, 32), size)] = piece[...]


def run_copies(copies):
    for copy in copies:
        copy.start()
    for copy in copies:
        copy.wait()


def place_columns(core, own, got, out, done, others=()):
    width = own.shape[1]

    def place(left, right):
        run_copies(
            [
                pltpu.make_async_copy(part, out.at[:, pl.ds(k * width, width)], done.at[k])
                for k, part in enumerate((left, right))
            ]
            + list(others)
        )

    @pl.when(core == 0)
    def _():
        place(own, got)

    @pl.when(core != 0)
    def _():
        place(got, own)


def columns_body(ids, own, got, out, done):
    place_columns(bits(ids)[0], own, got, out, done)


def collect_body(ids, f0, f1, f2, f3, g0, g1, g2, g3, own, got, features, grads, out, done, moved):
    core, chip, _ = bits(ids)
    size = f0.shape[0]
    copies = [
        pltpu.make_async_copy(piece, to.at[block(chip ^ mask, size)], moved.at[4 * k + mask])
        for k, (to, parts) in enumerate(((features, (f0, f1, f2, f3)), (grads, (g0, g1, g2, g3))))
        for mask, piece in enumerate(parts)
    ]
    place_columns(core, own, got, out, done, copies)


def pieces(field, chip):
    size = field.shape[0] // 4
    return [lax.dynamic_slice_in_dim(field, (chip ^ mask) * size, size, 0) for mask in range(4)]


def over_chips(parts):
    return [parts[0]] + [swap(parts[mask], "hi", 2 * mask) for mask in range(1, 4)]


def family_shards(track, near_weight, far_weight, cotangent):
    return family_step(track, near_weight, far_weight, cotangent)


def family_step(track, near_weight, far_weight, cotangent):
    rows, width = track.shape
    n_hi = lax.axis_size("hi")
    n_lo = lax.axis_size("lo")
    size = rows // 4
    half = width // 2
    tall = near_weight.shape[0]
    part = tall // n_lo
    hi = lax.axis_index("hi")
    lo = lax.axis_index("lo")
    ids = jnp.stack([hi, lo])
    chip = lax.shift_right_logical(hi, 1)
    scale = 1.0 / float(rows * n_hi * n_lo) ** 0.5
    full, piece = (rows, width), (size, width)
    padded = (rows + 2 * size, width)

    own = over_chips(pieces(track, chip))
    other = [swap(own[mask], "hi", 1) for mask in range(4)]
    out = hbm_call(
        weights_body, [(near_weight.shape, BF16)] * 4 + [(piece, F32)] * 4, (pltpu.HBM, pltpu.VMEM),
        ids, (near_weight, far_weight, cotangent),
        [pltpu.VMEM((8, tall // 4, width), F32), pltpu.SemaphoreType.DMA((8,)), pltpu.SemaphoreType.DMA((4,))], 8,
    )
    near_h, near_l, far_h, far_l = out[:4]
    cot = over_chips(out[4:])
    near_w, far_w = (near_h, near_l), (far_h, far_l)
    out = call(
        forward_body,
        [(piece, F32)] * 4 + [(full, F32)] * 2 + [(full, BF16)] * 2 + [(padded, BF16)] * 4,
        ids, *own, *other, *near_w, *far_w, scratch=[(full, F32)], room=16,
    )
    feats, slope_near, slope_far = over_chips(out[:4]), out[4], out[5]
    hid, own_pair, oth_pair = out[6:8], out[8:10], out[10:12]
    cot, g_h, g_l, far_other = call(
        far_other_body, [(full, F32), (full, BF16), (full, BF16), ((tall, half), F32)],
        ids, *cot, slope_far, *hid,
    )
    far_got = swap(far_other, "hi", 1)
    halves = [((n_lo, part // 2, half), F32)] * 2
    far_keep, far_send = call(
        far_own_body, halves, ids, *hid, g_h, g_l, far_got, scratch=[((tall, half), F32)], room=12
    )
    far_got = plane_swap(far_send, 0)
    grad, gn, gn_h, gn_l = call(
        backward_body, [(full, F32), (full, F32), (full, BF16), (full, BF16)],
        ids, cot, g_h, g_l, *far_w, slope_near,
    )
    gn_got = swap(gn, "hi", 1)
    (near_term,) = call(near_mine_body, [((tall, half), F32)], ids, *own_pair, *oth_pair, gn_h, gn_l)
    near_keep, near_send = call(
        near_both_body, halves, ids, near_term, *own_pair, *oth_pair, gn_got,
        scratch=[((tall, half), F32)], room=12,
    )
    near_got = plane_swap(near_send, 0)
    grads = call(
        track_body, [(piece, F32)] * 4, ids, grad, gn_h, gn_l, gn_got, *near_w,
        scratch=[(padded, BF16), (padded, BF16), (full, F32)], room=12,
    )
    grads = over_chips(grads)

    def scaled_total(*refs):
        total_body(scale, *refs)

    def lo_sum(kept, got):
        one = [(kept.shape[1:], F32)]
        parts = call(pick_body, one * 4, ids, kept, got)
        parts = [parts[0]] + [swap(parts[mask], "lo", mask) for mask in (1, 2, 3)]
        return call(scaled_total, one, ids, *parts)[0]

    far_mine = lo_sum(far_keep, far_got)
    wide_half = [((part // 2, half), F32)]
    (far_mine,) = call(cross_body, wide_half, ids, far_mine, plane_swap(far_mine, 1))
    rows_all = [((part, half), F32)]
    (rows_far,) = call(far_rows_body, rows_all, ids, far_mine, plane_swap(far_mine, 0))
    far_cols = swap(rows_far, "hi", 1)
    quarters = [((n_lo, part // 4, half), F32)] * 2
    near_keep, near_send = call(plane_body, quarters, ids, near_keep, near_got)
    near_mine = lo_sum(near_keep, plane_swap(near_send, 1))
    near_all = over_chips([near_mine] * 4)
    (rows_near,) = call(near_rows_body, rows_all, ids, *near_all)
    near_cols = swap(rows_near, "hi", 1)
    to_hbm = (pltpu.VMEM, pltpu.HBM)
    to_hbm = (pltpu.VMEM, pltpu.HBM)
    wide = ((part, width), F32)
    sems = [pltpu.SemaphoreType.DMA((2,))]
    features, grad_track, grad_far = hbm_call(
        collect_body, [(full, F32)] * 2 + [wide], to_hbm, ids, (*feats, *grads, rows_far, far_cols),
        sems + [pltpu.SemaphoreType.DMA((8,))], 2,
    )
    (grad_near,) = hbm_call(columns_body, [wide], to_hbm, ids, (rows_near, near_cols), sems, 2)
    return features, grad_track, grad_near, grad_far


def from_behind(value, axis, steps):
    count = lax.axis_size(axis)
    initial, last = (max(0, -steps), min(count, count - steps))
    return lax.ppermute(value, axis, [(source, source + steps) for source in range(initial, last)])


def halo_shards(track, tight_weight, wide_weight, cotangent):
    def near_pair(field):
        return from_behind(field, ("hi", "lo"), NEAR_STEPS), from_behind(field, ("hi", "lo"), -NEAR_STEPS)

    def far_pair(field):
        return from_behind(field, "hi", FAR_STEPS), from_behind(field, "hi", -FAR_STEPS)

    def back_product(before, center, after, weights):
        width = center.shape[1]
        total = dot(after, weights[0:width], (1, 1))
        total = total + dot(center, weights[width : 2 * width], (1, 1))
        return total + dot(before, weights[2 * width : 3 * width], (1, 1))

    near_prev, near_next = near_pair(track)
    track_taps = jnp.concatenate([near_prev, track, near_next], axis=1)
    pre_near = dot(track_taps, tight_weight, (1, 0))
    act_near, near_pull = jax.vjp(gelu_fn, pre_near)
    hidden = track + act_near
    far_prev, far_next = far_pair(hidden)
    hidden_taps = jnp.concatenate([far_prev, hidden, far_next], axis=1)
    pre_far = dot(hidden_taps, wide_weight, (1, 0))
    act_far, far_pull = jax.vjp(gelu_fn, pre_far)
    features = hidden + act_far
    g_far = far_pull(cotangent)[0]
    term_far = dot(hidden_taps, g_far, (0, 0))
    gfar_prev, gfar_next = far_pair(g_far)
    grad_hidden = cotangent + back_product(gfar_prev, g_far, gfar_next, wide_weight)
    g_near = near_pull(grad_hidden)[0]
    term_near = dot(track_taps, g_near, (0, 0))
    gnear_prev, gnear_next = near_pair(g_near)
    grad_track = grad_hidden + back_product(gnear_prev, g_near, gnear_next, tight_weight)
    scale = 1.0 / jnp.sqrt(jnp.float32(track.shape[0] * lax.axis_size("hi") * lax.axis_size("lo")))
    summed_near, summed_far = lax.psum((term_near, term_far), "hi")
    rows_near = lax.psum_scatter(summed_near, "lo", scatter_dimension=0, tiled=True)
    rows_far = lax.psum_scatter(summed_far, "lo", scatter_dimension=0, tiled=True)
    return (features, grad_track, rows_near * scale, rows_far * scale)


def solution(mesh):
    n_hi, n_lo = mesh.shape["hi"], mesh.shape["lo"]

    def step(track, tight_weight, wide_weight, cotangent):
        rows = track.shape[0] // (n_hi * n_lo)
        closed = NEAR_STEPS == n_lo and FAR_STEPS == 2 and n_hi == 8
        closed = closed and rows % (8 * n_hi) == 0 and tight_weight.shape[0] % (64 * n_lo) == 0
        closed = closed and tight_weight.shape[1] % 256 == 0
        if closed:
            shards = family_shards
        else:
            shards = halo_shards
        in_specs = (P(("hi", "lo"), None), P(), P(), P(("hi", "lo"), None))
        out_specs = (P(("hi", "lo"), None), P(("hi", "lo"), None), P("lo", None), P("lo", None))
        mapped = jax.shard_map(shards, mesh=mesh, in_specs=in_specs, out_specs=out_specs, check_vma=False)
        return mapped(track, tight_weight, wide_weight, cotangent)

    return step
```

```python
import jax
import jax.numpy as jnp
from jax import lax
from jax.experimental import pallas as pl
from jax.experimental.pallas import tpu as pltpu
from jax.sharding import PartitionSpec as P


NEAR_STEPS = 4
FAR_STEPS = 2
HP = lax.Precision.HIGH
F32 = jnp.float32
BF16 = jnp.bfloat16


def dot(a, b, contract):
    return lax.dot_general(
        a, b, ((contract[:1], contract[1:]), ((), ())), precision=HP, preferred_element_type=jnp.float32
    )


def gelu_fn(value):
    return jax.nn.gelu(value, approximate=True)


def call(body, outs, *args, scratch=(), to_hbm=False, room=4):
    vmem = pl.BlockSpec(memory_space=pltpu.VMEM)
    make = jax.ShapeDtypeStruct if to_hbm else pltpu.VMEM
    return pl.pallas_call(
        body,
        out_shape=[make(shape, dtype) for shape, dtype in outs],
        in_specs=[vmem] * len(args),
        out_specs=[vmem] * len(outs),
        scratch_shapes=[pltpu.VMEM(shape, dtype) for shape, dtype in scratch],
        compiler_params=pltpu.CompilerParams(vmem_limit_bytes=room * 1024 * 1024),
    )(*[pltpu.with_memory_space_constraint(arg, pltpu.VMEM) for arg in args])


def swap(value, axis, mask):
    count = lax.axis_size(axis)
    return lax.ppermute(value, axis, [(i, i ^ mask) for i in range(count)])


def plane_swap(value, turn):
    count = lax.axis_size("hi")
    return lax.ppermute(value, "hi", [(i, i ^ (2 << (i + turn) % 2)) for i in range(count)])


def bits():
    hi = lax.axis_index("hi")
    return hi & 1, hi >> 1, lax.axis_index("lo")


def turns(core, chip):
    return (chip >> core) & 1, (chip >> (1 - core)) & 1


def split(value):
    high = value.astype(BF16)
    return high, (value - high.astype(F32)).astype(BF16)


def mul(a, b, contract):
    dims = ((contract[:1], contract[1:]), ((), ()))

    def one(left, right):
        return lax.dot_general(left, right, dims, preferred_element_type=F32)

    return one(a[0], b[0]) + (one(a[0], b[1]) + one(a[1], b[0]))


def rows_of(pair, start, size):
    return tuple(ref[start : start + size] for ref in pair)


def gelu_both(u):
    root = 0.7978845608028654
    square = u * u
    tanh = jnp.tanh(root * (u + 0.044715 * (u * square)))
    half = 0.5 * (1.0 + tanh)
    slope = half + 0.5 * u * (1.0 - tanh * tanh) * (root * (1.0 + 3.0 * 0.044715 * square))
    return u * half, slope


def block(index, size):
    return pl.ds(pl.multiple_of(index * size, size), size)


def weights_body(near, far, cot, near_h, near_l, far_h, far_l, c0, c1, c2, c3, staged, done, moved):
    chip = bits()[1]
    parts, rows, _ = staged.shape
    each = parts // 2
    size = c0.shape[0]
    cuts = [
        pltpu.make_async_copy(cot.at[block(chip ^ mask, size)], out, moved.at[mask])
        for mask, out in enumerate((c0, c1, c2, c3))
    ]
    copies = [
        pltpu.make_async_copy((near, far)[k // each].at[pl.ds(k % each * rows, rows)], staged.at[k], done.at[k])
        for k in range(parts)
    ]
    for copy in copies[:each] + cuts + copies[each:]:
        copy.start()
    for k in range(parts):
        copies[k].wait()
        start = k % each * rows
        high, low = ((near_h, near_l), (far_h, far_l))[k // each]
        high[start : start + rows], low[start : start + rows] = split(staged[k])
    for copy in cuts:
        copy.wait()


def hbm_call(body, outs, specs, args, scratch, room):
    places = {pltpu.HBM: pl.BlockSpec(memory_space=pltpu.HBM), pltpu.VMEM: pl.BlockSpec(memory_space=pltpu.VMEM)}
    ins, out_place = specs
    return pl.pallas_call(
        body,
        out_shape=[out_place(shape, dtype) for shape, dtype in outs],
        in_specs=[places[ins]] * len(args),
        out_specs=[places[out_place]] * len(outs),
        scratch_shapes=scratch,
        compiler_params=pltpu.CompilerParams(vmem_limit_bytes=room * 1024 * 1024),
    )(*[pltpu.with_memory_space_constraint(arg, ins) for arg in args])


def forward_body(p0, p1, p2, p3, q0, q1, q2, q3, near_h, near_l, far_h, far_l,
                 f0, f1, f2, f3, slope_near, slope_far, hid_h, hid_l, own_h, own_l, oth_h, oth_l, field):
    core, chip, _ = bits()
    rows, width = slope_near.shape
    size = rows // 4
    pad = jnp.zeros((size, width), BF16)
    for ref in (own_h, own_l, oth_h, oth_l):
        ref[0:size] = pad
        ref[rows + size :] = pad
    for mask, (own, other) in enumerate(((p0, q0), (p1, q1), (p2, q2), (p3, q3))):
        field[block(chip ^ mask, size)] = own[...]
        high, low = split(other[...])
        oth_h[block((chip ^ mask) + 1, size)] = high
        oth_l[block((chip ^ mask) + 1, size)] = low
    track = field[...]
    own_h[size : rows + size], own_l[size : rows + size] = split(track)
    before = pl.ds(pl.multiple_of(core * size, size), rows)
    after = pl.ds(pl.multiple_of(core * size + size, size), rows)
    pre = mul(rows_of((own_h, own_l), size, rows), rows_of((near_h, near_l), width, width), (1, 0))
    pre = pre + mul((oth_h[before], oth_l[before]), rows_of((near_h, near_l), 0, width), (1, 0))
    pre = pre + mul((oth_h[after], oth_l[after]), rows_of((near_h, near_l), 2 * width, width), (1, 0))
    act, slope = gelu_both(pre)
    slope_near[...] = slope
    hidden = track + act
    hid_h[...], hid_l[...] = split(hidden)
    field[...] = mul((hid_h[...], hid_l[...]), rows_of((far_h, far_l), width, width), (1, 0))
    rest = rows - size
    field[size:] += mul(rows_of((hid_h, hid_l), 0, rest), rows_of((far_h, far_l), 0, width), (1, 0))
    field[0:rest] += mul(rows_of((hid_h, hid_l), size, rest), rows_of((far_h, far_l), 2 * width, width), (1, 0))
    act, slope = gelu_both(field[...])
    slope_far[...] = slope
    field[...] = hidden + act
    for mask, out in enumerate((f0, f1, f2, f3)):
        out[...] = field[block(chip ^ mask, size)]


def half_columns(pair, index):
    width = pair[0].shape[1] // 2
    return tuple(jnp.where(index == 0, ref[:, :width].astype(F32), ref[:, width:].astype(F32)).astype(BF16) for ref in pair)


def far_term(hid, grad, store):
    rows, _ = hid[0].shape
    size = rows // 4
    rest = rows - size
    store(0, mul(rows_of(hid, 0, rest), tuple(g[size:] for g in grad), (0, 0)))
    store(1, mul(tuple(h[...] for h in hid), grad, (0, 0)))
    store(2, mul(rows_of(hid, size, rest), tuple(g[:rest] for g in grad), (0, 0)))


def near_term(core, center, sides, grad, store):
    rows = grad[0].shape[0]
    size = rows // 4
    before = pl.ds(pl.multiple_of(core * size, size), rows)
    after = pl.ds(pl.multiple_of(core * size + size, size), rows)
    store(0, mul(tuple(ref[before] for ref in sides), grad, (0, 0)))
    store(1, mul(rows_of(center, size, rows), grad, (0, 0)))
    store(2, mul(tuple(ref[after] for ref in sides), grad, (0, 0)))


def far_other_body(c0, c1, c2, c3, slope, hid_h, hid_l, cot, g_h, g_l, term):
    core, chip, _ = bits()
    rows, width = cot.shape
    size = rows // 4
    for mask, piece in enumerate((c0, c1, c2, c3)):
        cot[block(chip ^ mask, size)] = piece[...]
    g_h[...], g_l[...] = split(cot[...] * slope[...])

    def store(tap, value):
        term[tap * width : (tap + 1) * width] = value

    far_term((hid_h, hid_l), half_columns((g_h, g_l), 1 - core), store)


def halve(total, bit, keep, send):
    count, half, _ = keep.shape
    for z in range(count):
        keep[z] = total[pl.ds(pl.multiple_of((2 * z + bit) * half, 32), half)]
        send[z] = total[pl.ds(pl.multiple_of((2 * z + 1 - bit) * half, 32), half)]


def far_own_body(hid_h, hid_l, g_h, g_l, got, keep, send, total):
    core, chip, _ = bits()
    width = hid_h.shape[1]

    def store(tap, value):
        total[tap * width : (tap + 1) * width] = value + got[tap * width : (tap + 1) * width]

    far_term((hid_h, hid_l), half_columns((g_h, g_l), core), store)
    halve(total, turns(core, chip)[0], keep, send)


def backward_body(cot, g_h, g_l, far_h, far_l, slope, grad, gn, gn_h, gn_l):
    rows, width = cot.shape
    size = rows // 4
    rest = rows - size
    grad[...] = cot[...] + mul((g_h[...], g_l[...]), rows_of((far_h, far_l), width, width), (1, 1))
    grad[0:rest] += mul(rows_of((g_h, g_l), size, rest), rows_of((far_h, far_l), 0, width), (1, 1))
    grad[size:] += mul(rows_of((g_h, g_l), 0, rest), rows_of((far_h, far_l), 2 * width, width), (1, 1))
    value = grad[...] * slope[...]
    gn[...] = value
    gn_h[...], gn_l[...] = split(value)


def near_mine_body(own_h, own_l, oth_h, oth_l, gn_h, gn_l, term):
    core, _, _ = bits()
    width = own_h.shape[1]

    def store(tap, value):
        term[tap * width : (tap + 1) * width] = value

    near_term(core, (own_h, own_l), (oth_h, oth_l), half_columns((gn_h, gn_l), core), store)


def near_both_body(term, own_h, own_l, oth_h, oth_l, other, keep, send, total):
    core, chip, _ = bits()
    width = own_h.shape[1]
    half = width // 2

    def store(tap, value):
        total[tap * width : (tap + 1) * width] = value + term[tap * width : (tap + 1) * width]

    grad = split(jnp.where(core == 0, other[:, :half], other[:, half:]))
    near_term(1 - core, (oth_h, oth_l), (own_h, own_l), grad, store)
    halve(total, turns(core, chip)[0], keep, send)


def track_body(grad, gn_h, gn_l, other, near_h, near_l, t0, t1, t2, t3, oth_h, oth_l, field):
    core, chip, _ = bits()
    rows, width = grad.shape
    size = rows // 4
    pad = jnp.zeros((size, width), BF16)
    for ref in (oth_h, oth_l):
        ref[0:size] = pad
        ref[rows + size :] = pad
    high, low = split(other[...])
    oth_h[size : rows + size] = high
    oth_l[size : rows + size] = low
    before = pl.ds(pl.multiple_of(core * size, size), rows)
    after = pl.ds(pl.multiple_of(core * size + size, size), rows)
    total = grad[...] + mul((gn_h[...], gn_l[...]), rows_of((near_h, near_l), width, width), (1, 1))
    total = total + mul((oth_h[after], oth_l[after]), rows_of((near_h, near_l), 0, width), (1, 1))
    field[...] = total + mul((oth_h[before], oth_l[before]), rows_of((near_h, near_l), 2 * width, width), (1, 1))
    for mask, out in enumerate((t0, t1, t2, t3)):
        out[...] = field[block(chip ^ mask, size)]


def plane_body(kept, got, keep, send):
    core, chip, _ = bits()
    bit = turns(core, chip)[1]
    half = keep.shape[1]
    mine = pl.ds(pl.multiple_of(bit * half, 32), half)
    theirs = pl.ds(pl.multiple_of((1 - bit) * half, 32), half)
    keep[...] = kept[:, mine] + got[:, mine]
    send[...] = kept[:, theirs] + got[:, theirs]


def pick_body(kept, got, p0, p1, p2, p3):
    lo = bits()[2]
    for mask, out in enumerate((p0, p1, p2, p3)):
        out[...] = kept[lo ^ mask] + got[lo ^ mask]


def total_body(scale, p0, p1, p2, p3, out):
    out[...] = ((p0[...] + p1[...]) + (p2[...] + p3[...])) * scale


def cross_body(own, got, out):
    out[...] = own[...] + got[...]


def far_rows_body(own, got, out):
    core, chip, _ = bits()
    bit = turns(core, chip)[0]
    half = own.shape[0]
    out[pl.ds(pl.multiple_of(bit * half, 32), half)] = own[...]
    out[pl.ds(pl.multiple_of((1 - bit) * half, 32), half)] = got[...]


def near_rows_body(s0, s1, s2, s3, out):
    core, chip, _ = bits()
    size = s0.shape[0]
    for mask, piece in enumerate((s0, s1, s2, s3)):
        first, second = turns(core, chip ^ mask)
        out[pl.ds(pl.multiple_of((2 * first + second) * size, 32), size)] = piece[...]


def run_copies(copies):
    for copy in copies:
        copy.start()
    for copy in copies:
        copy.wait()


def collect_body(f0, f1, f2, f3, g0, g1, g2, g3, far, far_got, near, near_got,
                 features, grads, grad_far, grad_near, sems):
    core, chip, _ = bits()
    size = f0.shape[0]
    width = far.shape[1]
    copies = [
        (piece, to.at[block(chip ^ mask, size)])
        for to, parts in ((features, (f0, f1, f2, f3)), (grads, (g0, g1, g2, g3)))
        for mask, piece in enumerate(parts)
    ]

    def place(swapped):
        columns = [
            (part, out.at[:, pl.ds((k ^ swapped) * width, width)])
            for out, parts in ((grad_far, (far, far_got)), (grad_near, (near, near_got)))
            for k, part in enumerate(parts)
        ]
        run_copies(
            [pltpu.make_async_copy(*pair, sems.at[k]) for k, pair in enumerate(copies + columns)]
        )

    @pl.when(core == 0)
    def _():
        place(0)

    @pl.when(core != 0)
    def _():
        place(1)


def pieces(field, chip):
    size = field.shape[0] // 4
    return [lax.dynamic_slice_in_dim(field, (chip ^ mask) * size, size, 0) for mask in range(4)]


def over_chips(parts):
    return [parts[0]] + [swap(parts[mask], "hi", 2 * mask) for mask in range(1, 4)]


def family_shards(track, near_weight, far_weight, cotangent):
    return family_step(track, near_weight, far_weight, cotangent)


def family_step(track, near_weight, far_weight, cotangent):
    rows, width = track.shape
    n_hi = lax.axis_size("hi")
    n_lo = lax.axis_size("lo")
    size = rows // 4
    half = width // 2
    tall = near_weight.shape[0]
    part = tall // n_lo
    hi = lax.axis_index("hi")
    chip = lax.shift_right_logical(hi, 1)
    scale = 1.0 / float(rows * n_hi * n_lo) ** 0.5
    full, piece = (rows, width), (size, width)
    padded = (rows + 2 * size, width)

    own = over_chips(pieces(track, chip))
    other = [swap(own[mask], "hi", 1) for mask in range(4)]
    out = hbm_call(
        weights_body, [(near_weight.shape, BF16)] * 4 + [(piece, F32)] * 4, (pltpu.HBM, pltpu.VMEM),
        (near_weight, far_weight, cotangent),
        [pltpu.VMEM((8, tall // 4, width), F32), pltpu.SemaphoreType.DMA((8,)), pltpu.SemaphoreType.DMA((4,))], 8,
    )
    near_h, near_l, far_h, far_l = out[:4]
    cot = over_chips(out[4:])
    near_w, far_w = (near_h, near_l), (far_h, far_l)
    out = call(
        forward_body,
        [(piece, F32)] * 4 + [(full, F32)] * 2 + [(full, BF16)] * 2 + [(padded, BF16)] * 4,
        *own, *other, *near_w, *far_w, scratch=[(full, F32)], room=16,
    )
    feats, slope_near, slope_far = over_chips(out[:4]), out[4], out[5]
    hid, own_pair, oth_pair = out[6:8], out[8:10], out[10:12]
    cot, g_h, g_l, far_other = call(
        far_other_body, [(full, F32), (full, BF16), (full, BF16), ((tall, half), F32)],
        *cot, slope_far, *hid,
    )
    far_got = swap(far_other, "hi", 1)
    halves = [((n_lo, part // 2, half), F32)] * 2
    far_keep, far_send = call(far_own_body, halves, *hid, g_h, g_l, far_got, scratch=[((tall, half), F32)], room=12)
    far_got = plane_swap(far_send, 0)
    grad, gn, gn_h, gn_l = call(
        backward_body, [(full, F32), (full, F32), (full, BF16), (full, BF16)],
        cot, g_h, g_l, *far_w, slope_near,
    )
    gn_got = swap(gn, "hi", 1)
    (near_term,) = call(near_mine_body, [((tall, half), F32)], *own_pair, *oth_pair, gn_h, gn_l)
    near_keep, near_send = call(
        near_both_body, halves, near_term, *own_pair, *oth_pair, gn_got,
        scratch=[((tall, half), F32)], room=12,
    )
    near_got = plane_swap(near_send, 0)
    grads = call(
        track_body, [(piece, F32)] * 4, grad, gn_h, gn_l, gn_got, *near_w,
        scratch=[(padded, BF16), (padded, BF16), (full, F32)], room=12,
    )
    grads = over_chips(grads)

    def scaled_total(*refs):
        total_body(scale, *refs)

    def lo_sum(kept, got):
        one = [(kept.shape[1:], F32)]
        parts = call(pick_body, one * 4, kept, got)
        parts = [parts[0]] + [swap(parts[mask], "lo", mask) for mask in (1, 2, 3)]
        return call(scaled_total, one, *parts)[0]

    far_mine = lo_sum(far_keep, far_got)
    wide_half = [((part // 2, half), F32)]
    (far_mine,) = call(cross_body, wide_half, far_mine, plane_swap(far_mine, 1))
    rows_all = [((part, half), F32)]
    (rows_far,) = call(far_rows_body, rows_all, far_mine, plane_swap(far_mine, 0))
    far_cols = swap(rows_far, "hi", 1)
    quarters = [((n_lo, part // 4, half), F32)] * 2
    near_keep, near_send = call(plane_body, quarters, near_keep, near_got)
    near_mine = lo_sum(near_keep, plane_swap(near_send, 1))
    near_all = over_chips([near_mine] * 4)
    (rows_near,) = call(near_rows_body, rows_all, *near_all)
    near_cols = swap(rows_near, "hi", 1)
    wide = ((part, width), F32)
    features, grad_track, grad_far, grad_near = hbm_call(
        collect_body, [(full, F32)] * 2 + [wide] * 2, (pltpu.VMEM, pltpu.HBM),
        (*feats, *grads, rows_far, far_cols, rows_near, near_cols), [pltpu.SemaphoreType.DMA((12,))], 2,
    )
    return features, grad_track, grad_near, grad_far


def from_behind(value, axis, steps):
    count = lax.axis_size(axis)
    initial, last = (max(0, -steps), min(count, count - steps))
    return lax.ppermute(value, axis, [(source, source + steps) for source in range(initial, last)])


def halo_shards(track, tight_weight, wide_weight, cotangent):
    def near_pair(field):
        return from_behind(field, ("hi", "lo"), NEAR_STEPS), from_behind(field, ("hi", "lo"), -NEAR_STEPS)

    def far_pair(field):
        return from_behind(field, "hi", FAR_STEPS), from_behind(field, "hi", -FAR_STEPS)

    def back_product(before, center, after, weights):
        width = center.shape[1]
        total = dot(after, weights[0:width], (1, 1))
        total = total + dot(center, weights[width : 2 * width], (1, 1))
        return total + dot(before, weights[2 * width : 3 * width], (1, 1))

    near_prev, near_next = near_pair(track)
    track_taps = jnp.concatenate([near_prev, track, near_next], axis=1)
    pre_near = dot(track_taps, tight_weight, (1, 0))
    act_near, near_pull = jax.vjp(gelu_fn, pre_near)
    hidden = track + act_near
    far_prev, far_next = far_pair(hidden)
    hidden_taps = jnp.concatenate([far_prev, hidden, far_next], axis=1)
    pre_far = dot(hidden_taps, wide_weight, (1, 0))
    act_far, far_pull = jax.vjp(gelu_fn, pre_far)
    features = hidden + act_far
    g_far = far_pull(cotangent)[0]
    term_far = dot(hidden_taps, g_far, (0, 0))
    gfar_prev, gfar_next = far_pair(g_far)
    grad_hidden = cotangent + back_product(gfar_prev, g_far, gfar_next, wide_weight)
    g_near = near_pull(grad_hidden)[0]
    term_near = dot(track_taps, g_near, (0, 0))
    gnear_prev, gnear_next = near_pair(g_near)
    grad_track = grad_hidden + back_product(gnear_prev, g_near, gnear_next, tight_weight)
    scale = 1.0 / jnp.sqrt(jnp.float32(track.shape[0] * lax.axis_size("hi") * lax.axis_size("lo")))
    summed_near, summed_far = lax.psum((term_near, term_far), "hi")
    rows_near = lax.psum_scatter(summed_near, "lo", scatter_dimension=0, tiled=True)
    rows_far = lax.psum_scatter(summed_far, "lo", scatter_dimension=0, tiled=True)
    return (features, grad_track, rows_near * scale, rows_far * scale)


def solution(mesh):
    n_hi, n_lo = mesh.shape["hi"], mesh.shape["lo"]

    def step(track, tight_weight, wide_weight, cotangent):
        rows = track.shape[0] // (n_hi * n_lo)
        closed = NEAR_STEPS == n_lo and FAR_STEPS == 2 and n_hi == 8
        closed = closed and rows % (8 * n_hi) == 0 and tight_weight.shape[0] % (64 * n_lo) == 0
        closed = closed and tight_weight.shape[1] % 256 == 0
        if closed:
            shards = family_shards
        else:
            shards = halo_shards
        in_specs = (P(("hi", "lo"), None), P(), P(), P(("hi", "lo"), None))
        out_specs = (P(("hi", "lo"), None), P(("hi", "lo"), None), P("lo", None), P("lo", None))
        mapped = jax.shard_map(shards, mesh=mesh, in_specs=in_specs, out_specs=out_specs, check_vma=False)
        return mapped(track, tight_weight, wide_weight, cotangent)

    return step
```

```python
import jax
import jax.numpy as jnp
from jax import lax
from jax.experimental import pallas as pl
from jax.experimental.pallas import tpu as pltpu
from jax.sharding import PartitionSpec as P


NEAR_STEPS = 4
FAR_STEPS = 2
HP = lax.Precision.HIGH
F32 = jnp.float32
BF16 = jnp.bfloat16


def dot(a, b, contract):
    return lax.dot_general(
        a, b, ((contract[:1], contract[1:]), ((), ())), precision=HP, preferred_element_type=jnp.float32
    )


def gelu_fn(value):
    return jax.nn.gelu(value, approximate=True)


def call(body, outs, *args, scratch=(), to_hbm=False, room=4):
    vmem = pl.BlockSpec(memory_space=pltpu.VMEM)
    make = jax.ShapeDtypeStruct if to_hbm else pltpu.VMEM
    return pl.pallas_call(
        body,
        out_shape=[make(shape, dtype) for shape, dtype in outs],
        in_specs=[vmem] * len(args),
        out_specs=[vmem] * len(outs),
        scratch_shapes=[pltpu.VMEM(shape, dtype) for shape, dtype in scratch],
        compiler_params=pltpu.CompilerParams(vmem_limit_bytes=room * 1024 * 1024),
    )(*[pltpu.with_memory_space_constraint(arg, pltpu.VMEM) for arg in args])


def swap(value, axis, mask):
    count = lax.axis_size(axis)
    return lax.ppermute(value, axis, [(i, i ^ mask) for i in range(count)])


def plane_swap(value, turn):
    count = lax.axis_size("hi")
    return lax.ppermute(value, "hi", [(i, i ^ (2 << (i + turn) % 2)) for i in range(count)])


def bits():
    hi = lax.axis_index("hi")
    return hi & 1, hi >> 1, lax.axis_index("lo")


def turns(core, chip):
    return (chip >> core) & 1, (chip >> (1 - core)) & 1


def split(value):
    high = value.astype(BF16)
    return high, (value - high.astype(F32)).astype(BF16)


def mul(a, b, contract):
    dims = ((contract[:1], contract[1:]), ((), ()))

    def one(left, right):
        return lax.dot_general(left, right, dims, preferred_element_type=F32)

    return one(a[0], b[0]) + (one(a[0], b[1]) + one(a[1], b[0]))


def rows_of(pair, start, size):
    return tuple(ref[start : start + size] for ref in pair)


def gelu_both(u):
    root = 0.7978845608028654
    square = u * u
    tanh = jnp.tanh(root * (u + 0.044715 * (u * square)))
    half = 0.5 * (1.0 + tanh)
    slope = half + 0.5 * u * (1.0 - tanh * tanh) * (root * (1.0 + 3.0 * 0.044715 * square))
    return u * half, slope


def block(index, size):
    return pl.ds(pl.multiple_of(index * size, size), size)


def weights_body(near, far, cot, near_h, near_l, far_h, far_l, c0, c1, c2, c3, staged, done, moved):
    chip = bits()[1]
    parts, rows, _ = staged.shape
    each = parts // 2
    size = c0.shape[0]
    cuts = [
        pltpu.make_async_copy(cot.at[block(chip ^ mask, size)], out, moved.at[mask])
        for mask, out in enumerate((c0, c1, c2, c3))
    ]
    copies = [
        pltpu.make_async_copy((near, far)[k // each].at[pl.ds(k % each * rows, rows)], staged.at[k], done.at[k])
        for k in range(parts)
    ]
    for copy in copies[:each] + cuts + copies[each:]:
        copy.start()
    for k in range(parts):
        copies[k].wait()
        start = k % each * rows
        high, low = ((near_h, near_l), (far_h, far_l))[k // each]
        high[start : start + rows], low[start : start + rows] = split(staged[k])
    for copy in cuts:
        copy.wait()


def hbm_call(body, outs, specs, args, scratch, room):
    places = {pltpu.HBM: pl.BlockSpec(memory_space=pltpu.HBM), pltpu.VMEM: pl.BlockSpec(memory_space=pltpu.VMEM)}
    ins, out_place = specs
    return pl.pallas_call(
        body,
        out_shape=[out_place(shape, dtype) for shape, dtype in outs],
        in_specs=[places[ins]] * len(args),
        out_specs=[places[out_place]] * len(outs),
        scratch_shapes=scratch,
        compiler_params=pltpu.CompilerParams(vmem_limit_bytes=room * 1024 * 1024),
    )(*[pltpu.with_memory_space_constraint(arg, ins) for arg in args])


def forward_body(p0, p1, p2, p3, q0, q1, q2, q3, near_h, near_l, far_h, far_l,
                 f0, f1, f2, f3, slope_near, slope_far, hid_h, hid_l, own_h, own_l, oth_h, oth_l, field):
    core, chip, _ = bits()
    rows, width = slope_near.shape
    size = rows // 4
    pad = jnp.zeros((size, width), BF16)
    for ref in (own_h, own_l, oth_h, oth_l):
        ref[0:size] = pad
        ref[rows + size :] = pad
    for mask, (own, other) in enumerate(((p0, q0), (p1, q1), (p2, q2), (p3, q3))):
        field[block(chip ^ mask, size)] = own[...]
        high, low = split(other[...])
        oth_h[block((chip ^ mask) + 1, size)] = high
        oth_l[block((chip ^ mask) + 1, size)] = low
    track = field[...]
    own_h[size : rows + size], own_l[size : rows + size] = split(track)
    before = pl.ds(pl.multiple_of(core * size, size), rows)
    after = pl.ds(pl.multiple_of(core * size + size, size), rows)
    pre = mul(rows_of((own_h, own_l), size, rows), rows_of((near_h, near_l), width, width), (1, 0))
    pre = pre + mul((oth_h[before], oth_l[before]), rows_of((near_h, near_l), 0, width), (1, 0))
    pre = pre + mul((oth_h[after], oth_l[after]), rows_of((near_h, near_l), 2 * width, width), (1, 0))
    act, slope = gelu_both(pre)
    slope_near[...] = slope
    hidden = track + act
    hid_h[...], hid_l[...] = split(hidden)
    field[...] = mul((hid_h[...], hid_l[...]), rows_of((far_h, far_l), width, width), (1, 0))
    rest = rows - size
    field[size:] += mul(rows_of((hid_h, hid_l), 0, rest), rows_of((far_h, far_l), 0, width), (1, 0))
    field[0:rest] += mul(rows_of((hid_h, hid_l), size, rest), rows_of((far_h, far_l), 2 * width, width), (1, 0))
    act, slope = gelu_both(field[...])
    slope_far[...] = slope
    field[...] = hidden + act
    for mask, out in enumerate((f0, f1, f2, f3)):
        out[...] = field[block(chip ^ mask, size)]


def half_columns(pair, index):
    width = pair[0].shape[1] // 2
    return tuple(jnp.where(index == 0, ref[:, :width].astype(F32), ref[:, width:].astype(F32)).astype(BF16) for ref in pair)


def far_term(hid, grad, store):
    rows, _ = hid[0].shape
    size = rows // 4
    rest = rows - size
    store(0, mul(rows_of(hid, 0, rest), tuple(g[size:] for g in grad), (0, 0)))
    store(1, mul(tuple(h[...] for h in hid), grad, (0, 0)))
    store(2, mul(rows_of(hid, size, rest), tuple(g[:rest] for g in grad), (0, 0)))


def near_term(core, center, sides, grad, store):
    rows = grad[0].shape[0]
    size = rows // 4
    before = pl.ds(pl.multiple_of(core * size, size), rows)
    after = pl.ds(pl.multiple_of(core * size + size, size), rows)
    store(0, mul(tuple(ref[before] for ref in sides), grad, (0, 0)))
    store(1, mul(rows_of(center, size, rows), grad, (0, 0)))
    store(2, mul(tuple(ref[after] for ref in sides), grad, (0, 0)))


def far_other_body(c0, c1, c2, c3, slope, hid_h, hid_l, cot, g_h, g_l, term):
    core, chip, _ = bits()
    rows, width = cot.shape
    size = rows // 4
    for mask, piece in enumerate((c0, c1, c2, c3)):
        cot[block(chip ^ mask, size)] = piece[...]
    g_h[...], g_l[...] = split(cot[...] * slope[...])

    def store(tap, value):
        term[tap * width : (tap + 1) * width] = value

    far_term((hid_h, hid_l), half_columns((g_h, g_l), 1 - core), store)


def halve(total, outs):
    core, chip, lo = bits()
    bit = turns(core, chip)[0]
    for pair, masks in ((outs[:2], (3, 2)), (outs[2:], (1, 0))):
        keep, send = pair
        half = keep.shape[1]
        for k, mask in enumerate(masks):
            start = (lo ^ mask) * 2 * half
            keep[k] = total[pl.ds(pl.multiple_of(start + bit * half, 32), half)]
            send[k] = total[pl.ds(pl.multiple_of(start + (1 - bit) * half, 32), half)]


def far_own_body(hid_h, hid_l, g_h, g_l, got, keep_a, send_a, keep_b, send_b, total):
    core, _, _ = bits()
    width = hid_h.shape[1]

    def store(tap, value):
        total[tap * width : (tap + 1) * width] = value + got[tap * width : (tap + 1) * width]

    far_term((hid_h, hid_l), half_columns((g_h, g_l), core), store)
    halve(total, (keep_a, send_a, keep_b, send_b))


def backward_body(cot, g_h, g_l, far_h, far_l, slope, grad, gn, gn_h, gn_l):
    rows, width = cot.shape
    size = rows // 4
    rest = rows - size
    grad[...] = cot[...] + mul((g_h[...], g_l[...]), rows_of((far_h, far_l), width, width), (1, 1))
    grad[0:rest] += mul(rows_of((g_h, g_l), size, rest), rows_of((far_h, far_l), 0, width), (1, 1))
    grad[size:] += mul(rows_of((g_h, g_l), 0, rest), rows_of((far_h, far_l), 2 * width, width), (1, 1))
    value = grad[...] * slope[...]
    gn[...] = value
    gn_h[...], gn_l[...] = split(value)


def near_mine_body(own_h, own_l, oth_h, oth_l, gn_h, gn_l, term):
    core, _, _ = bits()
    width = own_h.shape[1]

    def store(tap, value):
        term[tap * width : (tap + 1) * width] = value

    near_term(core, (own_h, own_l), (oth_h, oth_l), half_columns((gn_h, gn_l), core), store)


def near_both_body(term, own_h, own_l, oth_h, oth_l, other, keep_a, send_a, keep_b, send_b, total):
    core, _, _ = bits()
    width = own_h.shape[1]
    half = width // 2

    def store(tap, value):
        total[tap * width : (tap + 1) * width] = value + term[tap * width : (tap + 1) * width]

    grad = split(jnp.where(core == 0, other[:, :half], other[:, half:]))
    near_term(1 - core, (oth_h, oth_l), (own_h, own_l), grad, store)
    halve(total, (keep_a, send_a, keep_b, send_b))


def track_body(grad, gn_h, gn_l, other, near_h, near_l, t0, t1, t2, t3, oth_h, oth_l, field):
    core, chip, _ = bits()
    rows, width = grad.shape
    size = rows // 4
    pad = jnp.zeros((size, width), BF16)
    for ref in (oth_h, oth_l):
        ref[0:size] = pad
        ref[rows + size :] = pad
    high, low = split(other[...])
    oth_h[size : rows + size] = high
    oth_l[size : rows + size] = low
    before = pl.ds(pl.multiple_of(core * size, size), rows)
    after = pl.ds(pl.multiple_of(core * size + size, size), rows)
    total = grad[...] + mul((gn_h[...], gn_l[...]), rows_of((near_h, near_l), width, width), (1, 1))
    total = total + mul((oth_h[after], oth_l[after]), rows_of((near_h, near_l), 0, width), (1, 1))
    field[...] = total + mul((oth_h[before], oth_l[before]), rows_of((near_h, near_l), 2 * width, width), (1, 1))
    for mask, out in enumerate((t0, t1, t2, t3)):
        out[...] = field[block(chip ^ mask, size)]


def plane_body(kept, got, keep, send):
    core, chip, _ = bits()
    bit = turns(core, chip)[1]
    half = keep.shape[1]
    mine = pl.ds(pl.multiple_of(bit * half, 32), half)
    theirs = pl.ds(pl.multiple_of((1 - bit) * half, 32), half)
    keep[...] = kept[:, mine] + got[:, mine]
    send[...] = kept[:, theirs] + got[:, theirs]


def pair_body(kept, got, p0, p1):
    p0[...] = kept[0] + got[0]
    p1[...] = kept[1] + got[1]


def total_body(scale, p0, p1, p2, p3, out):
    out[...] = ((p0[...] + p1[...]) + (p2[...] + p3[...])) * scale


def cross_body(own, got, out):
    out[...] = own[...] + got[...]


def far_rows_body(own, got, out):
    core, chip, _ = bits()
    bit = turns(core, chip)[0]
    half = own.shape[0]
    out[pl.ds(pl.multiple_of(bit * half, 32), half)] = own[...]
    out[pl.ds(pl.multiple_of((1 - bit) * half, 32), half)] = got[...]


def near_rows_body(s0, s1, s2, s3, out):
    core, chip, _ = bits()
    size = s0.shape[0]
    for mask, piece in enumerate((s0, s1, s2, s3)):
        first, second = turns(core, chip ^ mask)
        out[pl.ds(pl.multiple_of((2 * first + second) * size, 32), size)] = piece[...]


def run_copies(copies):
    for copy in copies:
        copy.start()
    for copy in copies:
        copy.wait()


def collect_body(f0, f1, f2, f3, g0, g1, g2, g3, far, far_got, near, near_got,
                 features, grads, grad_far, grad_near, sems):
    core, chip, _ = bits()
    size = f0.shape[0]
    width = far.shape[1]
    copies = [
        (piece, to.at[block(chip ^ mask, size)])
        for to, parts in ((features, (f0, f1, f2, f3)), (grads, (g0, g1, g2, g3)))
        for mask, piece in enumerate(parts)
    ]

    def place(swapped):
        columns = [
            (part, out.at[:, pl.ds((k ^ swapped) * width, width)])
            for out, parts in ((grad_far, (far, far_got)), (grad_near, (near, near_got)))
            for k, part in enumerate(parts)
        ]
        run_copies(
            [pltpu.make_async_copy(*pair, sems.at[k]) for k, pair in enumerate(copies + columns)]
        )

    @pl.when(core == 0)
    def _():
        place(0)

    @pl.when(core != 0)
    def _():
        place(1)


def pieces(field, chip):
    size = field.shape[0] // 4
    return [lax.dynamic_slice_in_dim(field, (chip ^ mask) * size, size, 0) for mask in range(4)]


def over_chips(parts):
    return [parts[0]] + [swap(parts[mask], "hi", 2 * mask) for mask in range(1, 4)]


def family_shards(track, near_weight, far_weight, cotangent):
    return family_step(track, near_weight, far_weight, cotangent)


def family_step(track, near_weight, far_weight, cotangent):
    rows, width = track.shape
    n_hi = lax.axis_size("hi")
    n_lo = lax.axis_size("lo")
    size = rows // 4
    half = width // 2
    tall = near_weight.shape[0]
    part = tall // n_lo
    hi = lax.axis_index("hi")
    chip = lax.shift_right_logical(hi, 1)
    scale = 1.0 / float(rows * n_hi * n_lo) ** 0.5
    full, piece = (rows, width), (size, width)
    padded = (rows + 2 * size, width)

    own = over_chips(pieces(track, chip))
    other = [swap(own[mask], "hi", 1) for mask in range(4)]
    out = hbm_call(
        weights_body, [(near_weight.shape, BF16)] * 4 + [(piece, F32)] * 4, (pltpu.HBM, pltpu.VMEM),
        (near_weight, far_weight, cotangent),
        [pltpu.VMEM((8, tall // 4, width), F32), pltpu.SemaphoreType.DMA((8,)), pltpu.SemaphoreType.DMA((4,))], 8,
    )
    near_h, near_l, far_h, far_l = out[:4]
    cot = over_chips(out[4:])
    near_w, far_w = (near_h, near_l), (far_h, far_l)
    out = call(
        forward_body,
        [(piece, F32)] * 4 + [(full, F32)] * 2 + [(full, BF16)] * 2 + [(padded, BF16)] * 4,
        *own, *other, *near_w, *far_w, scratch=[(full, F32)], room=16,
    )
    feats, slope_near, slope_far = over_chips(out[:4]), out[4], out[5]
    hid, own_pair, oth_pair = out[6:8], out[8:10], out[10:12]
    cot, g_h, g_l, far_other = call(
        far_other_body, [(full, F32), (full, BF16), (full, BF16), ((tall, half), F32)],
        *cot, slope_far, *hid,
    )
    far_got = swap(far_other, "hi", 1)
    halves = [((2, part // 2, half), F32)] * 4
    far_q = call(far_own_body, halves, *hid, g_h, g_l, far_got, scratch=[((tall, half), F32)], room=12)
    far_a = far_q[0], plane_swap(far_q[1], 0)
    far_b = far_q[2], plane_swap(far_q[3], 0)
    grad, gn, gn_h, gn_l = call(
        backward_body, [(full, F32), (full, F32), (full, BF16), (full, BF16)],
        cot, g_h, g_l, *far_w, slope_near,
    )
    gn_got = swap(gn, "hi", 1)
    (near_term,) = call(near_mine_body, [((tall, half), F32)], *own_pair, *oth_pair, gn_h, gn_l)
    near_q = call(
        near_both_body, halves, near_term, *own_pair, *oth_pair, gn_got,
        scratch=[((tall, half), F32)], room=12,
    )
    near_a = near_q[0], plane_swap(near_q[1], 0)
    near_b = near_q[2], plane_swap(near_q[3], 0)
    grads = call(
        track_body, [(piece, F32)] * 4, grad, gn_h, gn_l, gn_got, *near_w,
        scratch=[(padded, BF16), (padded, BF16), (full, F32)], room=12,
    )
    grads = over_chips(grads)

    def scaled_total(*refs):
        total_body(scale, *refs)

    def lo_sum(pair_a, pair_b):
        one = [(pair_a[0].shape[1:], F32)]
        last, third = call(pair_body, one * 2, *pair_a)
        second, mine = call(pair_body, one * 2, *pair_b)
        parts = [swap(part, "lo", mask) for mask, part in ((1, second), (2, third), (3, last))]
        return call(scaled_total, one, mine, *parts)[0]

    far_mine = lo_sum(far_a, far_b)
    wide_half = [((part // 2, half), F32)]
    (far_mine,) = call(cross_body, wide_half, far_mine, plane_swap(far_mine, 1))
    rows_all = [((part, half), F32)]
    (rows_far,) = call(far_rows_body, rows_all, far_mine, plane_swap(far_mine, 0))
    far_cols = swap(rows_far, "hi", 1)
    quarters = [((2, part // 4, half), F32)] * 2

    def second_turn(pair):
        kept, send = call(plane_body, quarters, *pair)
        return kept, plane_swap(send, 1)

    near_mine = lo_sum(second_turn(near_a), second_turn(near_b))
    near_all = over_chips([near_mine] * 4)
    (rows_near,) = call(near_rows_body, rows_all, *near_all)
    near_cols = swap(rows_near, "hi", 1)
    wide = ((part, width), F32)
    features, grad_track, grad_far, grad_near = hbm_call(
        collect_body, [(full, F32)] * 2 + [wide] * 2, (pltpu.VMEM, pltpu.HBM),
        (*feats, *grads, rows_far, far_cols, rows_near, near_cols), [pltpu.SemaphoreType.DMA((12,))], 2,
    )
    return features, grad_track, grad_near, grad_far


def from_behind(value, axis, steps):
    count = lax.axis_size(axis)
    initial, last = (max(0, -steps), min(count, count - steps))
    return lax.ppermute(value, axis, [(source, source + steps) for source in range(initial, last)])


def halo_shards(track, tight_weight, wide_weight, cotangent):
    def near_pair(field):
        return from_behind(field, ("hi", "lo"), NEAR_STEPS), from_behind(field, ("hi", "lo"), -NEAR_STEPS)

    def far_pair(field):
        return from_behind(field, "hi", FAR_STEPS), from_behind(field, "hi", -FAR_STEPS)

    def back_product(before, center, after, weights):
        width = center.shape[1]
        total = dot(after, weights[0:width], (1, 1))
        total = total + dot(center, weights[width : 2 * width], (1, 1))
        return total + dot(before, weights[2 * width : 3 * width], (1, 1))

    near_prev, near_next = near_pair(track)
    track_taps = jnp.concatenate([near_prev, track, near_next], axis=1)
    pre_near = dot(track_taps, tight_weight, (1, 0))
    act_near, near_pull = jax.vjp(gelu_fn, pre_near)
    hidden = track + act_near
    far_prev, far_next = far_pair(hidden)
    hidden_taps = jnp.concatenate([far_prev, hidden, far_next], axis=1)
    pre_far = dot(hidden_taps, wide_weight, (1, 0))
    act_far, far_pull = jax.vjp(gelu_fn, pre_far)
    features = hidden + act_far
    g_far = far_pull(cotangent)[0]
    term_far = dot(hidden_taps, g_far, (0, 0))
    gfar_prev, gfar_next = far_pair(g_far)
    grad_hidden = cotangent + back_product(gfar_prev, g_far, gfar_next, wide_weight)
    g_near = near_pull(grad_hidden)[0]
    term_near = dot(track_taps, g_near, (0, 0))
    gnear_prev, gnear_next = near_pair(g_near)
    grad_track = grad_hidden + back_product(gnear_prev, g_near, gnear_next, tight_weight)
    scale = 1.0 / jnp.sqrt(jnp.float32(track.shape[0] * lax.axis_size("hi") * lax.axis_size("lo")))
    summed_near, summed_far = lax.psum((term_near, term_far), "hi")
    rows_near = lax.psum_scatter(summed_near, "lo", scatter_dimension=0, tiled=True)
    rows_far = lax.psum_scatter(summed_far, "lo", scatter_dimension=0, tiled=True)
    return (features, grad_track, rows_near * scale, rows_far * scale)


def solution(mesh):
    n_hi, n_lo = mesh.shape["hi"], mesh.shape["lo"]

    def step(track, tight_weight, wide_weight, cotangent):
        rows = track.shape[0] // (n_hi * n_lo)
        closed = NEAR_STEPS == n_lo and FAR_STEPS == 2 and n_hi == 8
        closed = closed and rows % (8 * n_hi) == 0 and tight_weight.shape[0] % (64 * n_lo) == 0
        closed = closed and tight_weight.shape[1] % 256 == 0
        if closed:
            shards = family_shards
        else:
            shards = halo_shards
        in_specs = (P(("hi", "lo"), None), P(), P(), P(("hi", "lo"), None))
        out_specs = (P(("hi", "lo"), None), P(("hi", "lo"), None), P("lo", None), P("lo", None))
        mapped = jax.shard_map(shards, mesh=mesh, in_specs=in_specs, out_specs=out_specs, check_vma=False)
        return mapped(track, tight_weight, wide_weight, cotangent)

    return step
```

```python
import jax
import jax.numpy as jnp
from jax import lax
from jax.experimental import pallas as pl
from jax.experimental.pallas import tpu as pltpu
from jax.sharding import PartitionSpec as P


NEAR_STEPS = 4
FAR_STEPS = 2
HP = lax.Precision.HIGH
F32 = jnp.float32
BF16 = jnp.bfloat16


def dot(a, b, contract):
    return lax.dot_general(
        a, b, ((contract[:1], contract[1:]), ((), ())), precision=HP, preferred_element_type=jnp.float32
    )


def gelu_fn(value):
    return jax.nn.gelu(value, approximate=True)


def call(body, outs, *args, scratch=(), to_hbm=False, room=4):
    vmem = pl.BlockSpec(memory_space=pltpu.VMEM)
    make = jax.ShapeDtypeStruct if to_hbm else pltpu.VMEM
    return pl.pallas_call(
        body,
        out_shape=[make(shape, dtype) for shape, dtype in outs],
        in_specs=[vmem] * len(args),
        out_specs=[vmem] * len(outs),
        scratch_shapes=[pltpu.VMEM(shape, dtype) for shape, dtype in scratch],
        compiler_params=pltpu.CompilerParams(vmem_limit_bytes=room * 1024 * 1024),
    )(*[pltpu.with_memory_space_constraint(arg, pltpu.VMEM) for arg in args])


def swap(value, axis, mask):
    count = lax.axis_size(axis)
    return lax.ppermute(value, axis, [(i, i ^ mask) for i in range(count)])


def plane_swap(value, turn):
    count = lax.axis_size("hi")
    return lax.ppermute(value, "hi", [(i, i ^ (2 << (i + turn) % 2)) for i in range(count)])


def bits():
    hi = lax.axis_index("hi")
    return hi & 1, hi >> 1, lax.axis_index("lo")


def turns(core, chip):
    return (chip >> core) & 1, (chip >> (1 - core)) & 1


def split(value):
    high = value.astype(BF16)
    return high, (value - high.astype(F32)).astype(BF16)


def mul(a, b, contract):
    dims = ((contract[:1], contract[1:]), ((), ()))

    def one(left, right):
        return lax.dot_general(left, right, dims, preferred_element_type=F32)

    return one(a[0], b[0]) + (one(a[0], b[1]) + one(a[1], b[0]))


def rows_of(pair, start, size):
    return tuple(ref[start : start + size] for ref in pair)


def gelu_both(u):
    root = 0.7978845608028654
    square = u * u
    tanh = jnp.tanh(root * (u + 0.044715 * (u * square)))
    half = 0.5 * (1.0 + tanh)
    slope = half + 0.5 * u * (1.0 - tanh * tanh) * (root * (1.0 + 3.0 * 0.044715 * square))
    return u * half, slope


def block(index, size):
    return pl.ds(pl.multiple_of(index * size, size), size)


def weights_body(near, far, cot, near_h, near_l, far_h, far_l, c0, c1, c2, c3, staged, done, moved):
    chip = bits()[1]
    parts, rows, _ = staged.shape
    each = parts // 2
    size = c0.shape[0]
    cuts = [
        pltpu.make_async_copy(cot.at[block(chip ^ mask, size)], out, moved.at[mask])
        for mask, out in enumerate((c0, c1, c2, c3))
    ]
    copies = [
        pltpu.make_async_copy((near, far)[k // each].at[pl.ds(k % each * rows, rows)], staged.at[k], done.at[k])
        for k in range(parts)
    ]
    for copy in copies[:each] + cuts + copies[each:]:
        copy.start()
    for k in range(parts):
        copies[k].wait()
        start = k % each * rows
        high, low = ((near_h, near_l), (far_h, far_l))[k // each]
        high[start : start + rows], low[start : start + rows] = split(staged[k])
    for copy in cuts:
        copy.wait()


def hbm_call(body, outs, specs, args, scratch, room):
    places = {pltpu.HBM: pl.BlockSpec(memory_space=pltpu.HBM), pltpu.VMEM: pl.BlockSpec(memory_space=pltpu.VMEM)}
    ins, out_place = specs
    return pl.pallas_call(
        body,
        out_shape=[out_place(shape, dtype) for shape, dtype in outs],
        in_specs=[places[ins]] * len(args),
        out_specs=[places[out_place]] * len(outs),
        scratch_shapes=scratch,
        compiler_params=pltpu.CompilerParams(vmem_limit_bytes=room * 1024 * 1024),
    )(*[pltpu.with_memory_space_constraint(arg, ins) for arg in args])


def forward_body(p0, p1, p2, p3, q0, q1, q2, q3, near_h, near_l, far_h, far_l,
                 f0, f1, f2, f3, slope_near, slope_far, hid_h, hid_l, own_h, own_l, oth_h, oth_l, field):
    core, chip, _ = bits()
    rows, width = slope_near.shape
    size = rows // 4
    pad = jnp.zeros((size, width), BF16)
    for ref in (own_h, own_l, oth_h, oth_l):
        ref[0:size] = pad
        ref[rows + size :] = pad
    for mask, (own, other) in enumerate(((p0, q0), (p1, q1), (p2, q2), (p3, q3))):
        field[block(chip ^ mask, size)] = own[...]
        high, low = split(other[...])
        oth_h[block((chip ^ mask) + 1, size)] = high
        oth_l[block((chip ^ mask) + 1, size)] = low
    track = field[...]
    own_h[size : rows + size], own_l[size : rows + size] = split(track)
    before = pl.ds(pl.multiple_of(core * size, size), rows)
    after = pl.ds(pl.multiple_of(core * size + size, size), rows)
    pre = mul(rows_of((own_h, own_l), size, rows), rows_of((near_h, near_l), width, width), (1, 0))
    pre = pre + mul((oth_h[before], oth_l[before]), rows_of((near_h, near_l), 0, width), (1, 0))
    pre = pre + mul((oth_h[after], oth_l[after]), rows_of((near_h, near_l), 2 * width, width), (1, 0))
    act, slope = gelu_both(pre)
    slope_near[...] = slope
    hidden = track + act
    hid_h[...], hid_l[...] = split(hidden)
    field[...] = mul((hid_h[...], hid_l[...]), rows_of((far_h, far_l), width, width), (1, 0))
    rest = rows - size
    field[size:] += mul(rows_of((hid_h, hid_l), 0, rest), rows_of((far_h, far_l), 0, width), (1, 0))
    field[0:rest] += mul(rows_of((hid_h, hid_l), size, rest), rows_of((far_h, far_l), 2 * width, width), (1, 0))
    act, slope = gelu_both(field[...])
    slope_far[...] = slope
    field[...] = hidden + act
    for mask, out in enumerate((f0, f1, f2, f3)):
        out[...] = field[block(chip ^ mask, size)]


def half_columns(pair, index):
    width = pair[0].shape[1] // 2
    return tuple(jnp.where(index == 0, ref[:, :width].astype(F32), ref[:, width:].astype(F32)).astype(BF16) for ref in pair)


def far_term(hid, grad, store):
    rows, _ = hid[0].shape
    size = rows // 4
    rest = rows - size
    store(0, mul(rows_of(hid, 0, rest), tuple(g[size:] for g in grad), (0, 0)))
    store(1, mul(tuple(h[...] for h in hid), grad, (0, 0)))
    store(2, mul(rows_of(hid, size, rest), tuple(g[:rest] for g in grad), (0, 0)))


def near_term(core, center, sides, grad, store):
    rows = grad[0].shape[0]
    size = rows // 4
    before = pl.ds(pl.multiple_of(core * size, size), rows)
    after = pl.ds(pl.multiple_of(core * size + size, size), rows)
    store(0, mul(tuple(ref[before] for ref in sides), grad, (0, 0)))
    store(1, mul(rows_of(center, size, rows), grad, (0, 0)))
    store(2, mul(tuple(ref[after] for ref in sides), grad, (0, 0)))


def far_other_body(c0, c1, c2, c3, slope, hid_h, hid_l, cot, g_h, g_l, term):
    core, chip, _ = bits()
    rows, width = cot.shape
    size = rows // 4
    for mask, piece in enumerate((c0, c1, c2, c3)):
        cot[block(chip ^ mask, size)] = piece[...]
    g_h[...], g_l[...] = split(cot[...] * slope[...])

    def store(tap, value):
        term[tap * width : (tap + 1) * width] = value

    far_term((hid_h, hid_l), half_columns((g_h, g_l), 1 - core), store)


def halve(total, outs):
    core, chip, lo = bits()
    bit = turns(core, chip)[0]
    for pair, masks in ((outs[:2], (3, 2)), (outs[2:], (1, 0))):
        keep, send = pair
        half = keep.shape[1]
        for k, mask in enumerate(masks):
            start = (lo ^ mask) * 2 * half
            keep[k] = total[pl.ds(pl.multiple_of(start + bit * half, 32), half)]
            send[k] = total[pl.ds(pl.multiple_of(start + (1 - bit) * half, 32), half)]


def far_own_body(hid_h, hid_l, g_h, g_l, got, keep_a, send_a, keep_b, send_b, total):
    core, _, _ = bits()
    width = hid_h.shape[1]

    def store(tap, value):
        total[tap * width : (tap + 1) * width] = value + got[tap * width : (tap + 1) * width]

    far_term((hid_h, hid_l), half_columns((g_h, g_l), core), store)
    halve(total, (keep_a, send_a, keep_b, send_b))


def backward_body(cot, g_h, g_l, far_h, far_l, slope, grad, gn, gn_h, gn_l):
    rows, width = cot.shape
    size = rows // 4
    rest = rows - size
    grad[...] = cot[...] + mul((g_h[...], g_l[...]), rows_of((far_h, far_l), width, width), (1, 1))
    grad[0:rest] += mul(rows_of((g_h, g_l), size, rest), rows_of((far_h, far_l), 0, width), (1, 1))
    grad[size:] += mul(rows_of((g_h, g_l), 0, rest), rows_of((far_h, far_l), 2 * width, width), (1, 1))
    value = grad[...] * slope[...]
    gn[...] = value
    gn_h[...], gn_l[...] = split(value)


def near_mine_body(own_h, own_l, oth_h, oth_l, gn_h, gn_l, term):
    core, _, _ = bits()
    width = own_h.shape[1]

    def store(tap, value):
        term[tap * width : (tap + 1) * width] = value

    near_term(core, (own_h, own_l), (oth_h, oth_l), half_columns((gn_h, gn_l), core), store)


def near_both_body(term, own_h, own_l, oth_h, oth_l, other, keep_a, send_a, keep_b, send_b, total):
    core, _, _ = bits()
    width = own_h.shape[1]
    half = width // 2

    def store(tap, value):
        total[tap * width : (tap + 1) * width] = value + term[tap * width : (tap + 1) * width]

    grad = split(jnp.where(core == 0, other[:, :half], other[:, half:]))
    near_term(1 - core, (oth_h, oth_l), (own_h, own_l), grad, store)
    halve(total, (keep_a, send_a, keep_b, send_b))


def track_body(grad, gn_h, gn_l, other, near_h, near_l, t0, t1, t2, t3, oth_h, oth_l, field):
    core, chip, _ = bits()
    rows, width = grad.shape
    size = rows // 4
    pad = jnp.zeros((size, width), BF16)
    for ref in (oth_h, oth_l):
        ref[0:size] = pad
        ref[rows + size :] = pad
    high, low = split(other[...])
    oth_h[size : rows + size] = high
    oth_l[size : rows + size] = low
    before = pl.ds(pl.multiple_of(core * size, size), rows)
    after = pl.ds(pl.multiple_of(core * size + size, size), rows)
    total = grad[...] + mul((gn_h[...], gn_l[...]), rows_of((near_h, near_l), width, width), (1, 1))
    total = total + mul((oth_h[after], oth_l[after]), rows_of((near_h, near_l), 0, width), (1, 1))
    field[...] = total + mul((oth_h[before], oth_l[before]), rows_of((near_h, near_l), 2 * width, width), (1, 1))
    for mask, out in enumerate((t0, t1, t2, t3)):
        out[...] = field[block(chip ^ mask, size)]


def plane_body(kept, got, keep, send):
    core, chip, _ = bits()
    bit = turns(core, chip)[1]
    half = keep.shape[1]
    mine = pl.ds(pl.multiple_of(bit * half, 32), half)
    theirs = pl.ds(pl.multiple_of((1 - bit) * half, 32), half)
    keep[...] = kept[:, mine] + got[:, mine]
    send[...] = kept[:, theirs] + got[:, theirs]


def pair_body(kept, got, p0, p1):
    p0[...] = kept[0] + got[0]
    p1[...] = kept[1] + got[1]


def total_body(scale, p0, p1, p2, p3, out):
    out[...] = ((p0[...] + p1[...]) + (p2[...] + p3[...])) * scale


def cross_body(own, got, out):
    out[...] = own[...] + got[...]


def far_rows_body(own, got, out):
    core, chip, _ = bits()
    bit = turns(core, chip)[0]
    half = own.shape[0]
    out[pl.ds(pl.multiple_of(bit * half, 32), half)] = own[...]
    out[pl.ds(pl.multiple_of((1 - bit) * half, 32), half)] = got[...]


def near_rows_body(s0, s1, s2, s3, out):
    core, chip, _ = bits()
    size = s0.shape[0]
    for mask, piece in enumerate((s0, s1, s2, s3)):
        first, second = turns(core, chip ^ mask)
        out[pl.ds(pl.multiple_of((2 * first + second) * size, 32), size)] = piece[...]


def run_copies(copies):
    for copy in copies:
        copy.start()
    for copy in copies:
        copy.wait()


def fields_body(f0, f1, f2, f3, g0, g1, g2, g3, features, grads, sems):
    chip = bits()[1]
    size = f0.shape[0]
    run_copies(
        [
            pltpu.make_async_copy(piece, to.at[block(chip ^ mask, size)], sems.at[4 * k + mask])
            for k, (to, parts) in enumerate(((features, (f0, f1, f2, f3)), (grads, (g0, g1, g2, g3))))
            for mask, piece in enumerate(parts)
        ]
    )


def columns_body(far, far_got, near, near_got, grad_far, grad_near, sems):
    core = bits()[0]
    width = far.shape[1]

    def place(swapped):
        columns = [
            (part, out.at[:, pl.ds((k ^ swapped) * width, width)])
            for out, parts in ((grad_far, (far, far_got)), (grad_near, (near, near_got)))
            for k, part in enumerate(parts)
        ]
        run_copies([pltpu.make_async_copy(*pair, sems.at[k]) for k, pair in enumerate(columns)])

    @pl.when(core == 0)
    def _():
        place(0)

    @pl.when(core != 0)
    def _():
        place(1)


def pieces(field, chip):
    size = field.shape[0] // 4
    return [lax.dynamic_slice_in_dim(field, (chip ^ mask) * size, size, 0) for mask in range(4)]


def over_chips(parts):
    return [parts[0]] + [swap(parts[mask], "hi", 2 * mask) for mask in range(1, 4)]


def family_shards(track, near_weight, far_weight, cotangent):
    return family_step(track, near_weight, far_weight, cotangent)


def family_step(track, near_weight, far_weight, cotangent):
    rows, width = track.shape
    n_hi = lax.axis_size("hi")
    n_lo = lax.axis_size("lo")
    size = rows // 4
    half = width // 2
    tall = near_weight.shape[0]
    part = tall // n_lo
    hi = lax.axis_index("hi")
    chip = lax.shift_right_logical(hi, 1)
    scale = 1.0 / float(rows * n_hi * n_lo) ** 0.5
    full, piece = (rows, width), (size, width)
    padded = (rows + 2 * size, width)

    own = over_chips(pieces(track, chip))
    other = [swap(own[mask], "hi", 1) for mask in range(4)]
    out = hbm_call(
        weights_body, [(near_weight.shape, BF16)] * 4 + [(piece, F32)] * 4, (pltpu.HBM, pltpu.VMEM),
        (near_weight, far_weight, cotangent),
        [pltpu.VMEM((8, tall // 4, width), F32), pltpu.SemaphoreType.DMA((8,)), pltpu.SemaphoreType.DMA((4,))], 8,
    )
    near_h, near_l, far_h, far_l = out[:4]
    cot = over_chips(out[4:])
    near_w, far_w = (near_h, near_l), (far_h, far_l)
    out = call(
        forward_body,
        [(piece, F32)] * 4 + [(full, F32)] * 2 + [(full, BF16)] * 2 + [(padded, BF16)] * 4,
        *own, *other, *near_w, *far_w, scratch=[(full, F32)], room=16,
    )
    feats, slope_near, slope_far = over_chips(out[:4]), out[4], out[5]
    hid, own_pair, oth_pair = out[6:8], out[8:10], out[10:12]
    cot, g_h, g_l, far_other = call(
        far_other_body, [(full, F32), (full, BF16), (full, BF16), ((tall, half), F32)],
        *cot, slope_far, *hid,
    )
    far_got = swap(far_other, "hi", 1)
    halves = [((2, part // 2, half), F32)] * 4
    far_q = call(far_own_body, halves, *hid, g_h, g_l, far_got, scratch=[((tall, half), F32)], room=12)
    far_a = far_q[0], plane_swap(far_q[1], 0)
    far_b = far_q[2], plane_swap(far_q[3], 0)
    grad, gn, gn_h, gn_l = call(
        backward_body, [(full, F32), (full, F32), (full, BF16), (full, BF16)],
        cot, g_h, g_l, *far_w, slope_near,
    )
    gn_got = swap(gn, "hi", 1)
    (near_term,) = call(near_mine_body, [((tall, half), F32)], *own_pair, *oth_pair, gn_h, gn_l)
    near_q = call(
        near_both_body, halves, near_term, *own_pair, *oth_pair, gn_got,
        scratch=[((tall, half), F32)], room=12,
    )
    near_a = near_q[0], plane_swap(near_q[1], 0)
    near_b = near_q[2], plane_swap(near_q[3], 0)
    grads = call(
        track_body, [(piece, F32)] * 4, grad, gn_h, gn_l, gn_got, *near_w,
        scratch=[(padded, BF16), (padded, BF16), (full, F32)], room=12,
    )
    grads = over_chips(grads)

    def scaled_total(*refs):
        total_body(scale, *refs)

    def lo_sum(pair_a, pair_b):
        one = [(pair_a[0].shape[1:], F32)]
        last, third = call(pair_body, one * 2, *pair_a)
        second, mine = call(pair_body, one * 2, *pair_b)
        parts = [swap(part, "lo", mask) for mask, part in ((1, second), (2, third), (3, last))]
        return call(scaled_total, one, mine, *parts)[0]

    far_mine = lo_sum(far_a, far_b)
    wide_half = [((part // 2, half), F32)]
    (far_mine,) = call(cross_body, wide_half, far_mine, plane_swap(far_mine, 1))
    rows_all = [((part, half), F32)]
    (rows_far,) = call(far_rows_body, rows_all, far_mine, plane_swap(far_mine, 0))
    far_cols = swap(rows_far, "hi", 1)
    quarters = [((2, part // 4, half), F32)] * 2

    def second_turn(pair):
        kept, send = call(plane_body, quarters, *pair)
        return kept, plane_swap(send, 1)

    near_mine = lo_sum(second_turn(near_a), second_turn(near_b))
    near_all = over_chips([near_mine] * 4)
    (rows_near,) = call(near_rows_body, rows_all, *near_all)
    near_cols = swap(rows_near, "hi", 1)
    to_hbm = (pltpu.VMEM, pltpu.HBM)
    features, grad_track = hbm_call(
        fields_body, [(full, F32)] * 2, to_hbm, (*feats, *grads), [pltpu.SemaphoreType.DMA((8,))], 2
    )
    grad_far, grad_near = hbm_call(
        columns_body, [((part, width), F32)] * 2, to_hbm, (rows_far, far_cols, rows_near, near_cols),
        [pltpu.SemaphoreType.DMA((4,))], 2,
    )
    return features, grad_track, grad_near, grad_far


def from_behind(value, axis, steps):
    count = lax.axis_size(axis)
    initial, last = (max(0, -steps), min(count, count - steps))
    return lax.ppermute(value, axis, [(source, source + steps) for source in range(initial, last)])


def halo_shards(track, tight_weight, wide_weight, cotangent):
    def near_pair(field):
        return from_behind(field, ("hi", "lo"), NEAR_STEPS), from_behind(field, ("hi", "lo"), -NEAR_STEPS)

    def far_pair(field):
        return from_behind(field, "hi", FAR_STEPS), from_behind(field, "hi", -FAR_STEPS)

    def back_product(before, center, after, weights):
        width = center.shape[1]
        total = dot(after, weights[0:width], (1, 1))
        total = total + dot(center, weights[width : 2 * width], (1, 1))
        return total + dot(before, weights[2 * width : 3 * width], (1, 1))

    near_prev, near_next = near_pair(track)
    track_taps = jnp.concatenate([near_prev, track, near_next], axis=1)
    pre_near = dot(track_taps, tight_weight, (1, 0))
    act_near, near_pull = jax.vjp(gelu_fn, pre_near)
    hidden = track + act_near
    far_prev, far_next = far_pair(hidden)
    hidden_taps = jnp.concatenate([far_prev, hidden, far_next], axis=1)
    pre_far = dot(hidden_taps, wide_weight, (1, 0))
    act_far, far_pull = jax.vjp(gelu_fn, pre_far)
    features = hidden + act_far
    g_far = far_pull(cotangent)[0]
    term_far = dot(hidden_taps, g_far, (0, 0))
    gfar_prev, gfar_next = far_pair(g_far)
    grad_hidden = cotangent + back_product(gfar_prev, g_far, gfar_next, wide_weight)
    g_near = near_pull(grad_hidden)[0]
    term_near = dot(track_taps, g_near, (0, 0))
    gnear_prev, gnear_next = near_pair(g_near)
    grad_track = grad_hidden + back_product(gnear_prev, g_near, gnear_next, tight_weight)
    scale = 1.0 / jnp.sqrt(jnp.float32(track.shape[0] * lax.axis_size("hi") * lax.axis_size("lo")))
    summed_near, summed_far = lax.psum((term_near, term_far), "hi")
    rows_near = lax.psum_scatter(summed_near, "lo", scatter_dimension=0, tiled=True)
    rows_far = lax.psum_scatter(summed_far, "lo", scatter_dimension=0, tiled=True)
    return (features, grad_track, rows_near * scale, rows_far * scale)


def solution(mesh):
    n_hi, n_lo = mesh.shape["hi"], mesh.shape["lo"]

    def step(track, tight_weight, wide_weight, cotangent):
        rows = track.shape[0] // (n_hi * n_lo)
        closed = NEAR_STEPS == n_lo and FAR_STEPS == 2 and n_hi == 8
        closed = closed and rows % (8 * n_hi) == 0 and tight_weight.shape[0] % (64 * n_lo) == 0
        closed = closed and tight_weight.shape[1] % 256 == 0
        if closed:
            shards = family_shards
        else:
            shards = halo_shards
        in_specs = (P(("hi", "lo"), None), P(), P(), P(("hi", "lo"), None))
        out_specs = (P(("hi", "lo"), None), P(("hi", "lo"), None), P("lo", None), P("lo", None))
        mapped = jax.shard_map(shards, mesh=mesh, in_specs=in_specs, out_specs=out_specs, check_vma=False)
        return mapped(track, tight_weight, wide_weight, cotangent)

    return step
```
